128 devices in a mesh: prompt: 4 (over z_hi, core), resp: 32 (over y, x, z_lo).
Axes of the slice: x: 4, y: 4, z: 4 (z_hi: 2, z_lo: 2; z = z_hi * 2 + z_lo), core: 2. Of those that a mesh axis runs over, the one named last changes fastest.
Arguments:
- queries: bfloat16 [4, 4096, 8192], P('prompt', 'resp'), may hold values from -6 to 6
- resp_kv: bfloat16 [4, 4096, 2048], P('prompt', 'resp'), may hold values from -6 to 6
- resp_segments: int32 [4, 4096], P('prompt', 'resp'), may hold values from 0 to 7, never falling along the last dimension, each value on 1 to 896 neighbouring positions
- prefix_kv: bfloat16 [512, 8, 2048], P(('prompt', 'resp')), may hold values from -6 to 6
- tile_plan: int32 [512, 2], P(('prompt', 'resp')), may hold values from 0 to 127, as said below
- prompt_lengths: int32 [4], P('prompt'), may hold values from 8 to 1024
Outputs:
- attended: bfloat16 [4, 4096, 8192], P('prompt', 'resp')
The draws below stay inside these ranges and needn't reach their ends.
Inputs may be any that keep to these rules, and one draw needn't show every extreme that they name: `tile_plan`: column 0 is a group in 0 .. 3 and column 1 a place in 0 .. 127; each pair of group and place stands once; the 4 tiles of each device hold one tile of every group, in any order. `resp_segments`: response numbers never fall along a group's tokens; each response has 1 to 896 tokens.
All inputs are finite; a program needn't handle non-finite values.
Results may differ from the reference program's by a relative error of at most 0.0055.
Values may be sent and summed in bfloat16 or wider, within the bound.
A program may use at most 128 MiB of HBM per device.

```python
import math
import jax
import jax.numpy as jnp
import numpy as np
from jax import lax

H = 64
KVH = 8
HD = 128
ROWS = 128
TILE = 8
TPG = 1
GROUPS = 4
RTOK = 4096
SEGS = 8
TILES = 512
PMAX = 1024
N_RESP = 32
DEVICES = 128


def draw_queries(key, part):
    shape = (GROUPS, RTOK, H * HD)
    return jnp.clip(jax.random.normal(jax.random.fold_in(key, 11), shape, jnp.float32), -6.0, 6.0).astype(jnp.bfloat16)


def draw_prefix_kv(key, part):
    shape = (TILES, TILE, 2 * KVH * HD)
    return jnp.clip(jax.random.normal(jax.random.fold_in(key, 13), shape, jnp.float32), -6.0, 6.0).astype(jnp.bfloat16)


def draw_tile_plan(key, part):
    per_group = DEVICES * TPG
    slots = GROUPS * TPG
    places = jnp.stack([jax.random.permutation(jax.random.fold_in(key, 100 + g), per_group) for g in range(GROUPS)])
    places = jnp.transpose(places.reshape(GROUPS, DEVICES, TPG), (1, 0, 2)).reshape(DEVICES, slots)
    owners = jnp.broadcast_to(jnp.repeat(jnp.arange(GROUPS, dtype=jnp.int32), TPG)[None, :], (DEVICES, slots))
    shuffle_keys = jax.random.split(jax.random.fold_in(key, 5), DEVICES)
    shuffles = jax.vmap(lambda one: jax.random.permutation(one, slots))(shuffle_keys)
    owners = jnp.take_along_axis(owners, shuffles, axis=1)
    places = jnp.take_along_axis(places.astype(jnp.int32), shuffles, axis=1)
    return jnp.stack([owners, places], axis=-1).reshape(DEVICES * slots, 2).astype(jnp.int32)


def touch_ends(result, rng, low, high):
    spot = [jax.random.randint(jax.random.fold_in(rng, axis), (), 0, length) for axis, length in enumerate(result.shape)]
    main_axis = result.shape.index(max(result.shape))
    next_to = spot[:main_axis] + [(spot[main_axis] + 1) % result.shape[main_axis]] + spot[main_axis + 1:]
    return result.at[tuple(spot)].set(low).at[tuple(next_to)].set(high)


def steps_of(key, shape, shards, least, largest):
    level = 1.0
    for dim, shards_of in shards:
        heights = jax.random.uniform(jax.random.fold_in(jax.random.fold_in(key, 6), dim), (shards_of,), jnp.float32, least / len(shards), largest / len(shards))
        level = level * jnp.repeat(jnp.exp(heights), shape[dim] // shards_of).reshape((-1,) + (1,) * (len(shape) - 1 - dim))
    return level


def length_profile(count, total, bound, slope):
    portions = [(1 << 20) // math.isqrt(standing ** slope) + 1 for standing in range(2, count + 1)]
    spare, holding = total - bound - (count - 1), [1] * (count - 1)
    while spare > 0:
        free = [i for i in range(count - 1) if holding[i] < bound]
        mass, left = sum([portions[i] for i in free]), spare
        for i in free:
            more = min(bound - holding[i], max(1, left * portions[i] // mass), spare)
            holding[i] = holding[i] + more
            spare = spare - more
    return np.array([bound] + holding)


def uneven(stream_key, number_of, total, most, lean):
    if number_of == 2:
        one = jax.random.randint(stream_key, (), max(1, total - most), min(most, total - 1) + 1)
        return jnp.stack([one, total - one])
    lengths = jnp.asarray(length_profile(number_of, total, most, lean), jnp.int32)
    couples = (number_of - 1) // 2
    source_of, receiver = lengths[1:1 + 2 * couples:2], lengths[2:2 + 2 * couples:2]
    margin = jnp.minimum(source_of - 1, most - receiver)
    passed = jax.random.randint(jax.random.fold_in(stream_key, 1), (couples,), 0, 1 << 20) % (margin + 1)
    lengths = lengths.at[1:1 + 2 * couples:2].set(source_of - passed).at[2:2 + 2 * couples:2].set(receiver + passed)
    return lengths[jax.random.permutation(jax.random.fold_in(stream_key, 2), number_of)]


def bell_draw(key, dims, width, bound, cuts=(), kind=jnp.bfloat16):
    entries = width * jax.random.normal(key, dims, jnp.float32)
    if cuts:
        entries = entries * steps_of(key, dims, cuts, -0.22, 0.18)
    return jnp.clip(entries, -bound, bound).astype(kind)


def setup_inputs(seed: int = 0) -> dict:
    keys = jax.random.split(jax.random.key(seed), 7)
    queries = draw_queries(jax.random.fold_in(keys[6], 71), 0)
    resp_kv = bell_draw(keys[1], (GROUPS, RTOK, 2 * KVH * HD), 1.0, 6.0, ((0, 4), (1, 32)))
    resp_segments = jax.vmap(lambda own: jnp.searchsorted(jnp.cumsum(uneven(own, SEGS, RTOK, 7 * ROWS, 1)), jnp.arange(RTOK), side="right"))(jax.random.split(keys[2], GROUPS)).reshape((GROUPS, RTOK)).astype(jnp.int32)
    prefix_kv = draw_prefix_kv(jax.random.fold_in(keys[6], 71), 0)
    tile_plan = draw_tile_plan(jax.random.fold_in(keys[6], 71), 0)
    prompt_lengths = touch_ends(jax.random.randint(keys[5], (GROUPS,), TILE, PMAX + 1), jax.random.fold_in(keys[5], 1), TILE, PMAX).astype(jnp.int32)
    return {"queries": queries, "resp_kv": resp_kv, "resp_segments": resp_segments, "prefix_kv": prefix_kv, "tile_plan": tile_plan, "prompt_lengths": prompt_lengths}


NEG_FILL = -1.0e30


def reference(queries, resp_kv, resp_segments, prefix_kv, tile_plan, prompt_lengths):
    split = KVH * HD
    group_size = H // KVH
    score_scale = 1.0 / (HD ** 0.5)
    reach = 7
    order = jnp.argsort(tile_plan[:, 0], stable=True)
    tiles = prefix_kv[order]
    plan = tile_plan[order]
    per_group = TILES // GROUPS
    tiles = tiles.reshape(GROUPS, per_group * TILE, 2 * split)
    places = (plan[:, 1][:, None] * TILE + jnp.arange(TILE, dtype=jnp.int32)[None, :]).reshape(GROUPS, per_group * TILE)
    resp_pad = jnp.concatenate([jnp.zeros((GROUPS, reach * ROWS, 2 * split), resp_kv.dtype), resp_kv], axis=1)
    seg_pad = jnp.concatenate([jnp.full((GROUPS, reach * ROWS), -1, jnp.int32), resp_segments.astype(jnp.int32)], axis=1)

    def one_block(index):
        group = (index // N_RESP).astype(jnp.int32)
        block = (index % N_RESP).astype(jnp.int32)
        start = (block * ROWS).astype(jnp.int32)
        zero = jnp.zeros((), jnp.int32)
        query = lax.dynamic_slice(queries, (group, start, zero), (1, ROWS, H * HD))[0]
        near = lax.dynamic_slice(resp_pad, (group, start, zero), (1, (reach + 1) * ROWS, 2 * split))[0]
        near_seg = lax.dynamic_slice(seg_pad, (group, start), (1, (reach + 1) * ROWS))[0]
        own_seg = lax.dynamic_slice(resp_segments.astype(jnp.int32), (group, start), (1, ROWS))[0]
        prefix = lax.dynamic_index_in_dim(tiles, group, 0, keepdims=False)
        prefix_live = lax.dynamic_index_in_dim(places, group, 0, keepdims=False) < lax.dynamic_index_in_dim(prompt_lengths, group, 0, keepdims=False)
        key_vectors = jnp.concatenate([prefix[:, :split], near[:, :split]], axis=0).reshape(-1, KVH, HD)
        value_vectors = jnp.concatenate([prefix[:, split:], near[:, split:]], axis=0).reshape(-1, KVH, HD)
        query_pos = jnp.arange(ROWS, dtype=jnp.int32)
        key_pos = jnp.arange((reach + 1) * ROWS, dtype=jnp.int32) - reach * ROWS
        resp_visible = (near_seg[None, :] == own_seg[:, None]) & (key_pos[None, :] <= query_pos[:, None])
        visible = jnp.concatenate([jnp.broadcast_to(prefix_live[None, :], (ROWS, prefix.shape[0])), resp_visible], axis=1)
        query_head_rows = query.reshape(ROWS, KVH, group_size, HD).astype(jnp.float32)
        logit_scores = jnp.einsum("wcpo,lco->wcpl", query_head_rows, key_vectors.astype(jnp.float32)) * score_scale
        mask = visible[:, None, None, :]
        logit_scores = jnp.where(mask, logit_scores, NEG_FILL)
        top = jnp.max(logit_scores, axis=-1, keepdims=True)
        attention_weight = jnp.where(mask, jnp.exp(logit_scores - top), 0.0)
        total = jnp.sum(attention_weight, axis=-1)
        rounded_probs = lax.optimization_barrier(attention_weight.astype(jnp.bfloat16)).astype(jnp.float32)
        weighted_sum = jnp.einsum("luem,mut->luet", rounded_probs, value_vectors.astype(jnp.float32))
        return (weighted_sum / total[..., None]).reshape(ROWS, H * HD).astype(jnp.bfloat16)

    blocks = lax.map(one_block, jnp.arange(GROUPS * N_RESP, dtype=jnp.int32))
    return blocks.reshape(GROUPS, RTOK, H * HD)
```

```python
import functools
import math

import jax
import jax.numpy as jnp
from jax import lax
from jax.experimental import pallas as pl
from jax.experimental.pallas import tpu as pltpu
from jax.sharding import PartitionSpec as P

H = 64
KVH = 8
HD = 128
ROWS = 128
TILE = 8
WIDE = 2 * KVH * HD
PWIDE = WIDE + 128
NEG = -1e30
C = math.log2(math.e) / math.sqrt(HD)
MESH = pl.DeviceIdType.MESH
VMEM = pltpu.VMEM
G = 8


def sort_kernel(plan_ref, prefix_ref, seg_ref, tiles_ref, seg8_ref):
    for q in range(4):
        slot = jnp.int32(0)
        place = jnp.int32(0)
        for s in range(4):
            hit = plan_ref[s, 0] == q
            slot = jnp.where(hit, s, slot)
            place = jnp.where(hit, plan_ref[s, 1], place)
        tiles_ref[q, :, :WIDE] = prefix_ref[slot]
        tiles_ref[q, :, WIDE:] = jnp.full((TILE, 128), place, jnp.int32).astype(jnp.float32).astype(jnp.bfloat16)
    seg8_ref[...] = jnp.broadcast_to(seg_ref[...], (8, 128))


def sort_tiles(plan, prefix, seg):
    return pl.pallas_call(
        sort_kernel,
        out_shape=(
            jax.ShapeDtypeStruct((4, TILE, PWIDE), jnp.bfloat16),
            jax.ShapeDtypeStruct((8, 128), jnp.int32),
        ),
        in_specs=[
            pl.BlockSpec(memory_space=pltpu.SMEM),
            pl.BlockSpec(memory_space=VMEM),
            pl.BlockSpec(memory_space=VMEM),
        ],
        out_specs=(pl.BlockSpec(memory_space=VMEM), pl.BlockSpec(memory_space=VMEM)),
        name="sort_tiles",
    )(plan, prefix, seg)


NCOPY = 64


def main_kernel(
    len_ref, q_hbm, kv_hbm, seg_hbm, tiles_hbm, out_hbm,
    q_s, rbuf, sbuf, pbuf, m_s, l_s, acc_s, bias_s, o_s,
    send, recv, local,
):
    p = lax.axis_index("prompt")
    r = lax.axis_index("resp")
    z = lax.rem(r, 2)
    x = lax.rem(r // 2, 4)
    y = r // 8

    def at(yy, xx, zz):
        return lax.rem(yy + 4, 4) * 8 + lax.rem(xx + 4, 4) * 2 + zz

    def ring(d):
        return lax.rem(r + 32 + d, 32)

    partner = r + 1 - 2 * z
    xp, xm, yp, ym = at(y, x + 1, z), at(y, x - 1, z), at(y + 1, x, z), at(y - 1, x, z)
    c1, cm1, c3, cm3 = ring(2), ring(-2), ring(6), ring(-6)
    xto = lax.rem(r + 1 + 6 * z, 32)
    xfrom = lax.rem(r + 25 + 6 * z, 32)

    barrier = pltpu.get_barrier_semaphore()
    for k in range(1, 4):
        pl.semaphore_signal(barrier, inc=1, device_id={"prompt": lax.rem(p + k, 4)}, device_id_type=MESH)
    for d in (partner, xp, xm, yp, ym, c1, cm1, c3, cm3, xto, xfrom):
        pl.semaphore_signal(barrier, inc=1, device_id={"resp": d}, device_id_type=MESH)

    l_q = pltpu.make_async_copy(q_hbm, q_s, local.at[0])
    l_kv = pltpu.make_async_copy(kv_hbm, rbuf.at[0], local.at[1])
    l_seg = pltpu.make_async_copy(seg_hbm, sbuf.at[0], local.at[2])
    l_tile = pltpu.make_async_copy(tiles_hbm.at[p], pbuf.at[r, pl.ds(pl.multiple_of(p * 8, 8), 8)], local.at[3])
    l_tile.start()
    l_kv.start()
    l_seg.start()
    l_q.start()
    pl.semaphore_wait(barrier, 14)

    counter = [0]
    started = []

    def copy(src, dst, to):
        i = counter[0]
        counter[0] += 1
        assert i < NCOPY
        c = pltpu.make_async_remote_copy(
            src_ref=src, dst_ref=dst, send_sem=send.at[i], recv_sem=recv.at[i], device_id=to, device_id_type=MESH
        )
        started.append(c)
        return c

    def rs(d):
        return {"resp": d}

    lo, hi = pl.ds(0, 64), pl.ds(64, 64)
    p0 = []
    for k in range(1, 4):
        q = lax.rem(p + k, 4)
        p0.append(copy(tiles_hbm.at[q], pbuf.at[r, pl.ds(pl.multiple_of(p * 8, 8), 8)], {"prompt": q}))
    n1 = [copy(kv_hbm.at[h], rbuf.at[1, h], rs(c1)) for h in (lo, hi)]
    n3 = [copy(kv_hbm.at[h], rbuf.at[3, h], rs(c3)) for h in (lo, hi)]
    xx = [copy(kv_hbm.at[h], rbuf.at[7, h], rs(xto)) for h in (lo, hi)]
    n2 = [copy(rbuf.at[1, lo], rbuf.at[2, lo], rs(c1)), copy(rbuf.at[3, hi], rbuf.at[2, hi], rs(cm1))]
    m1 = [copy(rbuf.at[1, h], rbuf.at[4, h], rs(partner)) for h in (lo, hi)]
    m2 = [copy(rbuf.at[2, h], rbuf.at[5, h], rs(partner)) for h in (lo, hi)]
    m3 = [copy(rbuf.at[3, h], rbuf.at[6, h], rs(partner)) for h in (lo, hi)]
    s1 = copy(seg_hbm, sbuf.at[1], rs(c1))
    s3 = copy(seg_hbm, sbuf.at[3], rs(c3))
    s7 = copy(seg_hbm, sbuf.at[7], rs(xto))
    s2 = copy(sbuf.at[1], sbuf.at[2], rs(c1))
    s4 = copy(sbuf.at[1], sbuf.at[4], rs(partner))
    s5 = copy(sbuf.at[2], sbuf.at[5], rs(partner))
    s6 = copy(sbuf.at[3], sbuf.at[6], rs(partner))

    def pair(yy, xx_):
        return pbuf.at[pl.ds(at(yy, xx_, 0), 2)]

    def one(yy, xx_, zz):
        return pbuf.at[at(yy, xx_, zz)]

    pz = copy(pbuf.at[r], pbuf.at[r], rs(partner))
    pxa = copy(pair(y, x), pair(y, x), rs(xp))
    pxb = copy(pair(y, x), pair(y, x), rs(xm))
    pxc = copy(one(y, x - 1, 0), one(y, x - 1, 0), rs(xp))
    pxd = copy(one(y, x + 1, 1), one(y, x + 1, 1), rs(xm))
    offs = (0, -1, 1, 2)
    pya = [copy(pair(y, x + o), pair(y, x + o), rs(yp)) for o in offs]
    pyb = [copy(pair(y, x + o), pair(y, x + o), rs(ym)) for o in offs]
    pyc = [copy(pair(y - 1, x + o), pair(y - 1, x + o), rs(yp)) for o in offs[:2]]
    pyd = [copy(pair(y + 1, x + o), pair(y + 1, x + o), rs(ym)) for o in offs[2:]]

    def start(*cs):
        for c in cs:
            c.start()

    def got(*cs):
        for c in cs:
            c.wait_recv()

    start(*p0, s1, s3, s7, n1[0], n3[0])
    l_tile.wait()
    got(*p0)
    start(pz, xx[0])
    got(pz)
    start(pya[0], pyb[0], pxa, pxb, n1[1], n3[1], xx[1])
    l_kv.wait()
    l_seg.wait()
    l_q.wait()

    def relay0():
        got(s1, s3)
        start(s2, s4, s6)
        got(n1[0])
        start(n2[0], m1[0])
        got(n3[0])
        start(m3[0])

    def relay1():
        got(pxa)
        start(pya[1], pyb[1], pxc)
        got(pxb)
        start(pya[2], pyb[2], pxd)

    def relay2():
        got(n1[1], n3[1])
        start(n2[1], m1[1], m3[1])
        got(s2)
        start(s5)

    def relay3():
        got(pxc, pxd)
        start(pya[3], pyb[3])
        got(pya[0], n2[0])
        start(pyc[0], m2[0])

    def relay4():
        got(pya[1], n2[1])
        start(pyc[1], m2[1])
        got(pyb[0], pyb[1], pyb[2])
        start(pyd[0])

    def relay5():
        got(pyb[3])
        start(pyd[1])

    relay0()
    relay1()
    relay2()
    relay3()
    relay4()
    relay5()

    seg_own = jnp.transpose(jnp.broadcast_to(sbuf[0, 0:1].astype(jnp.float32), (128, 128)))
    row = lax.broadcasted_iota(jnp.int32, (128, 128), 0)
    col = lax.broadcasted_iota(jnp.int32, (128, 128), 1)

    def resp_bias(slots):
        for j, s in enumerate(slots):
            if s == 0:
                d = jnp.int32(0)
            elif s <= 3:
                d = jnp.int32(2 * s)
            elif s <= 6:
                d = 2 * (s - 3) - 1 + 2 * z
            else:
                d = 7 - 6 * z
            theirs = sbuf[s, 0:1].astype(jnp.float32)
            theirs = jnp.where(r >= d, theirs, -1.0)
            ok = seg_own == theirs
            if s == 0:
                ok = ok & (col <= row)
            bias_s[:, j * 128:(j + 1) * 128] = jnp.where(ok, 0.0, NEG)

    def prefix_bias(rows):
        limit = len_ref[0]
        hot = jnp.where(lax.broadcasted_iota(jnp.int32, (8, 128), 1) == 0, 1.0, 0.0).astype(jnp.bfloat16)
        for j, yy in enumerate(rows):
            marks = pbuf[pl.ds(yy * 8, 8), :, WIDE:].reshape(256, 128)
            places = lax.dot_general(hot, marks, (((1,), (1,)), ((), ())), preferred_element_type=jnp.float32)
            tok = lax.rem(lax.broadcasted_iota(jnp.int32, (1, 256), 1), 8)
            pos = places[0:1].astype(jnp.int32) * 8 + tok
            bias_s[:, j * 256:(j + 1) * 256] = jnp.broadcast_to(jnp.where(pos < limit, 0.0, NEG), (128, 256))

    def resp_cols(slots):
        def load(off):
            return jnp.concatenate([rbuf[s, :, pl.ds(off, 128)] for s in slots], axis=0)
        return load

    def prefix_cols(rows):
        def load(off):
            return jnp.concatenate([pbuf[pl.ds(yy * 8, 8), :, pl.ds(off, 128)].reshape(256, 128) for yy in rows], axis=0)
        return load

    nt = (((1,), (1,)), ((), ()))
    nn = (((1,), (0,)), ((), ()))

    def attend(load, first, last):
        def step(h, carry):
            off = pl.multiple_of(h * 128, 128)
            k = load(off)
            v = load(pl.multiple_of(off + KVH * HD, 128))
            bias = bias_s[...]
            for g0 in range(0, 8, G):
                def cols(g):
                    return pl.ds(pl.multiple_of(off * 8 + (g0 + g) * 128, 128), 128)
                qs = jnp.concatenate([q_s[:, cols(g)] for g in range(G)], axis=0)
                scores = lax.dot_general(qs, k, nt, preferred_element_type=jnp.float32)
                ps, als, lss = [], [], []
                for g in range(G):
                    n = h * 8 + g0 + g
                    s = scores[g * 128:(g + 1) * 128] + bias
                    parts = [s[:, j * 128:(j + 1) * 128] for j in range(4)]
                    mx = jnp.max(functools.reduce(jnp.maximum, parts), axis=1, keepdims=True)
                    if first:
                        m = jnp.broadcast_to(mx, (128, 128))
                    else:
                        mo = m_s[n]
                        m = jnp.maximum(mo, mx)
                        al = jnp.exp2((mo - m) * C)
                        als.append(al)
                    w = [jnp.exp2((t - m) * C) for t in parts]
                    ls = functools.reduce(lambda a, b: a + b, w)
                    if not first:
                        ls = ls + l_s[n] * al
                    lss.append(ls)
                    if not last:
                        m_s[n] = m
                        l_s[n] = ls
                    ps.append(jnp.concatenate([t.astype(jnp.bfloat16) for t in w], axis=1))
                pv_all = lax.dot_general(jnp.concatenate(ps, axis=0), v, nn, preferred_element_type=jnp.float32)
                for g in range(G):
                    n = h * 8 + g0 + g
                    pv = pv_all[g * 128:(g + 1) * 128]
                    if not first:
                        pv = pv + acc_s[n] * als[g]
                    if not last:
                        acc_s[n] = pv
                    else:
                        tot = jnp.sum(lss[g], axis=1, keepdims=True)
                        o_s[:, cols(g)] = (pv / tot).astype(jnp.bfloat16)
            return carry
        lax.fori_loop(0, KVH, step, 0)

    ra, rb = (0, 1, 3, 7), (4, 6, 2, 5)
    y0, y1, y2, y3 = y, lax.rem(y + 3, 4), lax.rem(y + 1, 4), lax.rem(y + 2, 4)

    got(*xx, s7)
    resp_bias(ra)
    attend(resp_cols(ra), True, False)
    got(pya[2], pya[3])
    prefix_bias((y0, y1))
    attend(prefix_cols((y0, y1)), False, False)
    got(*pyc, *pyd)
    prefix_bias((y2, y3))
    attend(prefix_cols((y2, y3)), False, False)
    got(*m1, *m2, *m3, s4, s5, s6)
    resp_bias(rb)
    attend(resp_cols(rb), False, True)
    done = pltpu.make_async_copy(o_s, out_hbm, local.at[4])
    done.start()
    for c in started:
        c.wait_send()
    done.wait()


def on_device(queries, resp_kv, resp_segments, prefix_kv, tile_plan, prompt_lengths):
    tiles, seg8 = sort_tiles(tile_plan, prefix_kv, resp_segments)
    anywhere = pl.BlockSpec(memory_space=pl.ANY)
    out = pl.pallas_call(
        main_kernel,
        out_shape=jax.ShapeDtypeStruct((ROWS, H * HD), jnp.bfloat16),
        in_specs=[pl.BlockSpec(memory_space=pltpu.SMEM)] + [anywhere] * 4,
        out_specs=anywhere,
        scratch_shapes=[
            VMEM((ROWS, H * HD), jnp.bfloat16),
            VMEM((8, ROWS, WIDE), jnp.bfloat16),
            VMEM((8, 8, 128), jnp.int32),
            VMEM((32, 32, PWIDE), jnp.bfloat16),
            VMEM((H, ROWS, 128), jnp.float32),
            VMEM((H, ROWS, 128), jnp.float32),
            VMEM((H, ROWS, 128), jnp.float32),
            VMEM((ROWS, 512), jnp.float32),
            VMEM((ROWS, H * HD), jnp.bfloat16),
            pltpu.SemaphoreType.DMA((NCOPY,)),
            pltpu.SemaphoreType.DMA((NCOPY,)),
            pltpu.SemaphoreType.DMA((5,)),
        ],
        compiler_params=pltpu.CompilerParams(
            collective_id=0, has_side_effects=True, vmem_limit_bytes=60 << 20
        ),
        name="attend",
    )(prompt_lengths, queries[0], resp_kv[0], seg8, tiles)
    return out[None]


def solution(mesh):
    return jax.shard_map(
        on_device,
        mesh=mesh,
        in_specs=(
            P("prompt", "resp", None),
            P("prompt", "resp", None),
            P("prompt", "resp"),
            P(("prompt", "resp"), None, None),
            P(("prompt", "resp"), None),
            P("prompt"),
        ),
        out_specs=P("prompt", "resp", None),
        check_vma=False,
    )
```

```python
import functools
import math

import jax
import jax.numpy as jnp
from jax import lax
from jax.experimental import pallas as pl
from jax.experimental.pallas import tpu as pltpu
from jax.sharding import PartitionSpec as P

H = 64
KVH = 8
HD = 128
ROWS = 128
TILE = 8
WIDE = 2 * KVH * HD
PWIDE = WIDE + 128
NEG = -1e30
C = math.log2(math.e) / math.sqrt(HD)
MESH = pl.DeviceIdType.MESH
VMEM = pltpu.VMEM
G = 8


def sort_kernel(plan_ref, prefix_ref, seg_ref, tiles_ref, seg8_ref):
    for q in range(4):
        slot = jnp.int32(0)
        place = jnp.int32(0)
        for s in range(4):
            hit = plan_ref[0, s] == q
            slot = jnp.where(hit, s, slot)
            place = jnp.where(hit, plan_ref[1, s], place)
        tiles_ref[q, :, :WIDE] = prefix_ref[slot]
        tiles_ref[q, :, WIDE:] = jnp.full((TILE, 128), place, jnp.int32).astype(jnp.float32).astype(jnp.bfloat16)
    seg8_ref[...] = jnp.broadcast_to(seg_ref[...], (8, 128))


def sort_tiles(plan, prefix, seg):
    return pl.pallas_call(
        sort_kernel,
        out_shape=(
            jax.ShapeDtypeStruct((4, TILE, PWIDE), jnp.bfloat16),
            jax.ShapeDtypeStruct((8, 128), jnp.int32),
        ),
        in_specs=[
            pl.BlockSpec(memory_space=pltpu.SMEM),
            pl.BlockSpec(memory_space=VMEM),
            pl.BlockSpec(memory_space=VMEM),
        ],
        out_specs=(pl.BlockSpec(memory_space=VMEM), pl.BlockSpec(memory_space=VMEM)),
        name="sort_tiles",
    )(plan, prefix, seg)


NCOPY = 64


def main_kernel(
    len_ref, q_hbm, kv_hbm, seg_hbm, tiles_hbm, out_hbm,
    q_s, rbuf, sbuf, pbuf, m_s, l_s, acc_s, bias_s, o_s,
    send, recv, local,
):
    p = lax.axis_index("prompt")
    r = lax.axis_index("resp")
    z = lax.rem(r, 2)
    x = lax.rem(r // 2, 4)
    y = r // 8

    def at(yy, xx, zz):
        return lax.rem(yy + 4, 4) * 8 + lax.rem(xx + 4, 4) * 2 + zz

    def ring(d):
        return lax.rem(r + 32 + d, 32)

    partner = r + 1 - 2 * z
    xp, xm, yp, ym = at(y, x + 1, z), at(y, x - 1, z), at(y + 1, x, z), at(y - 1, x, z)

    barrier = pltpu.get_barrier_semaphore()
    for k in range(1, 4):
        pl.semaphore_signal(barrier, inc=1, device_id={"prompt": lax.rem(p + k, 4)}, device_id_type=MESH)
    for d in (partner, xp, xm, yp, ym):
        pl.semaphore_signal(barrier, inc=1, device_id={"resp": d}, device_id_type=MESH)
    for k in range(1, 8):
        for d in (ring(k), ring(-k)):
            pl.semaphore_signal(barrier, inc=1, device_id={"resp": d}, device_id_type=MESH)

    l_q = pltpu.make_async_copy(q_hbm, q_s, local.at[0])
    l_kv = pltpu.make_async_copy(kv_hbm, rbuf.at[0], local.at[1])
    l_seg = pltpu.make_async_copy(seg_hbm, sbuf.at[0], local.at[2])
    l_tile = pltpu.make_async_copy(tiles_hbm.at[p], pbuf.at[r, pl.ds(pl.multiple_of(p * 8, 8), 8)], local.at[3])
    l_tile.start()
    l_kv.start()
    l_seg.start()
    l_q.start()
    l_kv.wait()
    pl.semaphore_wait(barrier, 22)

    counter = [0]
    started = []

    def copy(src, dst, to, when=None, recv_as=None):
        i = counter[0]
        counter[0] += 1
        assert i < NCOPY
        c = pltpu.make_async_remote_copy(
            src_ref=src, dst_ref=dst, send_sem=send.at[i], recv_sem=recv.at[i if recv_as is None else recv_as],
            device_id=to, device_id_type=MESH,
        )
        started.append((c, when))
        c_index[id(c)] = i
        return c

    c_index = {}

    def rs(d):
        return {"resp": d}

    def start(*cs, when=None):
        def go():
            for c in cs:
                c.start()
        if when is None:
            go()
        else:
            pl.when(when)(go)

    def got(*cs):
        for c in cs:
            c.wait_recv()

    halves = (pl.ds(0, 64), pl.ds(64, 64))
    OWN, ROWB = 0, 8
    p0 = []
    for k in range(1, 4):
        q = lax.rem(p + k, 4)
        p0.append(copy(tiles_hbm.at[q], pbuf.at[r, pl.ds(pl.multiple_of(p * 8, 8), 8)], {"prompt": q}))
    segs = [copy(seg_hbm, sbuf.at[k], rs(ring(k))) for k in range(1, 8)]
    src1 = jnp.where(x == 3, ROWB, OWN)
    src3 = jnp.where(x == 0, OWN, ROWB)
    src7 = jnp.where(z == 0, OWN, ROWB)
    tt = [copy(rbuf.at[OWN, h], rbuf.at[ROWB, h], rs(yp)) for h in halves]
    n1 = [copy(rbuf.at[src1, h], rbuf.at[1, h], rs(xp)) for h in halves]
    n3 = [copy(rbuf.at[src3, h], rbuf.at[3, h], rs(xm)) for h in halves]
    xx = [copy(rbuf.at[src7, h], rbuf.at[7, h], rs(partner)) for h in halves]
    m1 = [copy(rbuf.at[1, h], rbuf.at[4, h], rs(partner)) for h in halves]
    m3 = [copy(rbuf.at[3, h], rbuf.at[6, h], rs(partner)) for h in halves]
    lo, hi = halves
    n2 = [
        copy(rbuf.at[1, lo], rbuf.at[2, lo], rs(xp), when=x < 3),
        copy(rbuf.at[3, hi], rbuf.at[2, hi], rs(xm), when=x > 0),
    ]
    n2x = [
        copy(rbuf.at[3, lo], rbuf.at[2, lo], rs(xm), when=x == 1, recv_as=c_index[id(n2[0])]),
        copy(rbuf.at[1, hi], rbuf.at[2, hi], rs(xp), when=x == 2, recv_as=c_index[id(n2[1])]),
    ]
    m2 = [
        copy(rbuf.at[4, lo], rbuf.at[5, lo], rs(xp), when=x < 3),
        copy(rbuf.at[2, hi], rbuf.at[5, hi], rs(partner)),
    ]
    m2x = copy(rbuf.at[6, lo], rbuf.at[5, lo], rs(xm), when=x == 1, recv_as=c_index[id(m2[0])])

    def pair(yy, xx_):
        return pbuf.at[pl.ds(at(yy, xx_, 0), 2)]

    def one(yy, xx_, zz):
        return pbuf.at[at(yy, xx_, zz)]

    pz = copy(pbuf.at[r], pbuf.at[r], rs(partner))
    pxa = copy(pair(y, x), pair(y, x), rs(xp))
    pxb = copy(pair(y, x), pair(y, x), rs(xm))
    pxc = copy(one(y, x - 1, 0), one(y, x - 1, 0), rs(xp))
    pxd = copy(one(y, x + 1, 1), one(y, x + 1, 1), rs(xm))
    offs = (0, -1, 1, 2)
    pya = [copy(pair(y, x + o), pair(y, x + o), rs(yp)) for o in offs]
    pyb = [copy(pair(y, x + o), pair(y, x + o), rs(ym)) for o in offs]
    pyc = copy(pair(y - 1, x), pair(y - 1, x), rs(yp))
    pyd = [copy(pair(y + 1, x + o), pair(y + 1, x + o), rs(ym)) for o in offs[1:]]

    start(*p0, tt[0])
    start(n1[0], when=x < 3)
    start(n3[0], when=x == 0)
    start(*segs)
    l_tile.wait()
    got(*p0)
    start(pz)
    start(xx[0], when=z == 0)
    got(pz)
    start(pya[0], pyb[0], pxa, pxb, tt[1])
    start(n1[1], when=x < 3)
    start(n3[1], when=x == 0)
    start(xx[1], when=z == 0)
    l_seg.wait()
    l_q.wait()

    def relay_t(i):
        got(tt[i])
        start(n1[i], when=x == 3)
        start(n3[i], when=x > 0)
        start(xx[i], when=z == 1)

    def relay_pa():
        got(pxa)
        start(pya[1], pyb[1], pxc)

    def relay_pb():
        got(pxb)
        start(pya[2], pyb[2], pxd)

    def relay_pc():
        got(pxc, pxd)
        start(pya[3], pyb[3])

    def relay_n1(i):
        got(n1[i])
        if i == 0:
            start(n2[0], when=x < 3)
        else:
            start(n2x[1], when=x == 2)
        start(m1[i])

    def relay_n3(i):
        got(n3[i])
        if i == 0:
            start(n2x[0], when=x == 1)
        else:
            start(n2[1], when=x > 0)
        start(m3[i])

    def relay_m1():
        got(m1[0])
        start(m2[0], when=x < 3)

    def relay_m3():
        got(m3[0])
        start(m2x, when=x == 1)

    def relay_n2():
        got(n2[1])
        start(m2[1])

    def relay_yc():
        got(pya[0])
        start(pyc)

    def relay_yd(i):
        got(pyb[1 + i])
        start(pyd[i])

    seg_own = jnp.transpose(jnp.broadcast_to(sbuf[0, 0:1].astype(jnp.float32), (128, 128)))
    row = lax.broadcasted_iota(jnp.int32, (128, 128), 0)
    col = lax.broadcasted_iota(jnp.int32, (128, 128), 1)

    def resp_bias(slots):
        for j, s in slots:
            if s == 0:
                d = jnp.int32(0)
            elif s <= 3:
                d = jnp.int32(2 * s)
            elif s <= 6:
                d = 2 * (s - 3) - 1 + 2 * z
            else:
                d = 7 - 6 * z
            theirs = sbuf[d, 0:1].astype(jnp.float32)
            theirs = jnp.where(r >= d, theirs, -1.0)
            ok = seg_own == theirs
            if s == 0:
                ok = ok & (col <= row)
            bias_s[:, j * 128:(j + 1) * 128] = jnp.where(ok, 0.0, NEG)

    def prefix_bias(rows):
        limit = len_ref[0]
        hot = jnp.where(lax.broadcasted_iota(jnp.int32, (8, 128), 1) == 0, 1.0, 0.0).astype(jnp.bfloat16)
        for j, yy in rows:
            marks = pbuf[pl.ds(yy * 8, 8), :, WIDE:].reshape(256, 128)
            places = lax.dot_general(hot, marks, (((1,), (1,)), ((), ())), preferred_element_type=jnp.float32)
            tok = lax.rem(lax.broadcasted_iota(jnp.int32, (1, 256), 1), 8)
            pos = places[0:1].astype(jnp.int32) * 8 + tok
            bias_s[:, j * 128:j * 128 + 256] = jnp.broadcast_to(jnp.where(pos < limit, 0.0, NEG), (128, 256))

    def resp_cols(slots):
        def load(off):
            return jnp.concatenate([rbuf[s, :, pl.ds(off, 128)] for s in slots], axis=0)
        return load

    def prefix_cols(rows):
        def load(off):
            return jnp.concatenate([pbuf[pl.ds(yy * 8, 8), :, pl.ds(off, 128)].reshape(256, 128) for yy in rows], axis=0)
        return load

    nt = (((1,), (1,)), ((), ()))
    nn = (((1,), (0,)), ((), ()))

    def attend(load, width, first, last, hooks=()):
        def step(h, carry):
            for i, fns in hooks:
                def run(fns=fns):
                    for f in fns:
                        f()
                pl.when(h == i)(run)
            off = pl.multiple_of(h * 128, 128)
            k = load(off)
            v = load(pl.multiple_of(off + KVH * HD, 128))
            bias = bias_s[:, :width * 128]
            for g0 in range(0, 8, G):
                def cols(g):
                    return pl.ds(pl.multiple_of(off * 8 + (g0 + g) * 128, 128), 128)
                qs = jnp.concatenate([q_s[:, cols(g)] for g in range(G)], axis=0)
                scores = lax.dot_general(qs, k, nt, preferred_element_type=jnp.float32)
                ps, als, lss = [], [], []
                for g in range(G):
                    n = h * 8 + g0 + g
                    s = scores[g * 128:(g + 1) * 128] + bias
                    parts = [s[:, j * 128:(j + 1) * 128] for j in range(width)]
                    mx = jnp.max(functools.reduce(jnp.maximum, parts), axis=1, keepdims=True)
                    if first:
                        m = jnp.broadcast_to(mx, (128, 128))
                    else:
                        mo = m_s[n]
                        m = jnp.maximum(mo, mx)
                        al = jnp.exp2((mo - m) * C)
                        als.append(al)
                    w = [jnp.exp2((t - m) * C) for t in parts]
                    ls = functools.reduce(lambda a, b: a + b, w)
                    if not first:
                        ls = ls + l_s[n] * al
                    lss.append(ls)
                    if not last:
                        m_s[n] = m
                        l_s[n] = ls
                    ps.append(jnp.concatenate([t.astype(jnp.bfloat16) for t in w], axis=1))
                pv_all = lax.dot_general(jnp.concatenate(ps, axis=0), v, nn, preferred_element_type=jnp.float32)
                for g in range(G):
                    n = h * 8 + g0 + g
                    pv = pv_all[g * 128:(g + 1) * 128]
                    if not first:
                        pv = pv + acc_s[n] * als[g]
                    if not last:
                        acc_s[n] = pv
                    else:
                        tot = jnp.sum(lss[g], axis=1, keepdims=True)
                        o_s[:, cols(g)] = (pv / tot).astype(jnp.bfloat16)
            return carry
        lax.fori_loop(0, KVH, step, 0)

    y0, y1, y2, y3 = y, lax.rem(y + 3, 4), lax.rem(y + 1, 4), lax.rem(y + 2, 4)

    def both(slots, rows):
        loads = [resp_cols(slots)] if slots else []
        loads += [prefix_cols(rows)] if rows else []
        def load(off):
            return jnp.concatenate([f(off) for f in loads], axis=0) if len(loads) > 1 else loads[0](off)
        resp_bias(list(enumerate(slots)))
        prefix_bias([(len(slots) + 2 * i, yy) for i, yy in enumerate(rows)])
        return load, len(slots) + 2 * len(rows)

    relay_t(0)
    relay_pa()
    relay_pb()
    relay_n1(0)
    relay_t(1)
    relay_pc()
    load, width = both((0,), (y0,))
    attend(load, width, True, False, hooks=(
        (0, (lambda: relay_n3(0), lambda: relay_n1(1))),
        (2, (relay_yc, relay_m1)),
        (4, (lambda: relay_n3(1), lambda: relay_yd(0))),
        (6, (lambda: got(*xx, *segs), lambda: relay_yd(1), relay_m3)),
    ))
    load, width = both((1, 3, 7), ())
    attend(load, width, False, False, hooks=(
        (1, (relay_n2,)),
        (4, (lambda: relay_yd(2),)),
    ))
    got(*pya[1:], pyb[0])
    load, width = both((), (y1, y2))
    attend(load, width, False, False)
    got(m1[1], m3[1], n2[0])
    load, width = both((4, 6, 2), ())
    attend(load, width, False, False)
    got(pyc, *pyd, *m2)
    load, width = both((5,), (y3,))
    attend(load, width, False, True)
    done = pltpu.make_async_copy(o_s, out_hbm, local.at[4])
    done.start()
    for c, when in started:
        if when is None:
            c.wait_send()
        else:
            pl.when(when)(c.wait_send)
    done.wait()


def on_device(queries, resp_kv, resp_segments, prefix_kv, tile_plan, prompt_lengths):
    tiles, seg8 = sort_tiles(tile_plan.T, prefix_kv, resp_segments)
    anywhere = pl.BlockSpec(memory_space=pl.ANY)
    out = pl.pallas_call(
        main_kernel,
        out_shape=jax.ShapeDtypeStruct((ROWS, H * HD), jnp.bfloat16),
        in_specs=[pl.BlockSpec(memory_space=pltpu.SMEM)] + [anywhere] * 4,
        out_specs=anywhere,
        scratch_shapes=[
            VMEM((ROWS, H * HD), jnp.bfloat16),
            VMEM((9, ROWS, WIDE), jnp.bfloat16),
            VMEM((8, 8, 128), jnp.int32),
            VMEM((32, 32, PWIDE), jnp.bfloat16),
            VMEM((H, ROWS, 128), jnp.float32),
            VMEM((H, ROWS, 128), jnp.float32),
            VMEM((H, ROWS, 128), jnp.float32),
            VMEM((ROWS, 512), jnp.float32),
            VMEM((ROWS, H * HD), jnp.bfloat16),
            pltpu.SemaphoreType.DMA((NCOPY,)),
            pltpu.SemaphoreType.DMA((NCOPY,)),
            pltpu.SemaphoreType.DMA((5,)),
        ],
        compiler_params=pltpu.CompilerParams(
            collective_id=0, has_side_effects=True, vmem_limit_bytes=60 << 20
        ),
        name="attend",
    )(prompt_lengths, queries[0], resp_kv[0], seg8, tiles)
    return out[None]


def solution(mesh):
    return jax.shard_map(
        on_device,
        mesh=mesh,
        in_specs=(
            P("prompt", "resp", None),
            P("prompt", "resp", None),
            P("prompt", "resp"),
            P(("prompt", "resp"), None, None),
            P(("prompt", "resp"), None),
            P("prompt"),
        ),
        out_specs=P("prompt", "resp", None),
        check_vma=False,
    )
```

```python
import functools
import math

import jax
import jax.numpy as jnp
from jax import lax
from jax.experimental import pallas as pl
from jax.experimental.pallas import tpu as pltpu
from jax.sharding import PartitionSpec as P

H = 64
KVH = 8
HD = 128
ROWS = 128
TILE = 8
WIDE = 2 * KVH * HD
PWIDE = WIDE + 128
NEG = -1e30
C = math.log2(math.e) / math.sqrt(HD)
MESH = pl.DeviceIdType.MESH
VMEM = pltpu.VMEM
G = 8


def sort_kernel(plan_ref, prefix_ref, seg_ref, tiles_ref, seg8_ref):
    for q in range(4):
        slot = jnp.int32(0)
        place = jnp.int32(0)
        for s in range(4):
            hit = plan_ref[0, s] == q
            slot = jnp.where(hit, s, slot)
            place = jnp.where(hit, plan_ref[1, s], place)
        tiles_ref[q, :, :WIDE] = prefix_ref[slot]
        tiles_ref[q, :, WIDE:] = jnp.full((TILE, 128), place, jnp.int32).astype(jnp.float32).astype(jnp.bfloat16)
    seg8_ref[...] = jnp.broadcast_to(seg_ref[...], (8, 128))


def sort_tiles(plan, prefix, seg):
    return pl.pallas_call(
        sort_kernel,
        out_shape=(
            jax.ShapeDtypeStruct((4, TILE, PWIDE), jnp.bfloat16),
            jax.ShapeDtypeStruct((8, 128), jnp.int32),
        ),
        in_specs=[
            pl.BlockSpec(memory_space=pltpu.SMEM),
            pl.BlockSpec(memory_space=VMEM),
            pl.BlockSpec(memory_space=VMEM),
        ],
        out_specs=(pl.BlockSpec(memory_space=VMEM), pl.BlockSpec(memory_space=VMEM)),
        name="sort_tiles",
    )(plan, prefix, seg)


NCOPY = 64


def main_kernel(
    len_ref, q_hbm, kv_hbm, seg_hbm, tiles_hbm, out_hbm,
    q_s, rbuf, sbuf, pbuf, m_s, l_s, acc_s, bias_s, o_s,
    send, recv, local,
):
    p = lax.axis_index("prompt")
    r = lax.axis_index("resp")
    z = lax.rem(r, 2)
    x = lax.rem(r // 2, 4)
    y = r // 8

    def at(yy, xx, zz):
        return lax.rem(yy + 4, 4) * 8 + lax.rem(xx + 4, 4) * 2 + zz

    def ring(d):
        return lax.rem(r + 32 + d, 32)

    partner = r + 1 - 2 * z
    xp, xm, yp, ym = at(y, x + 1, z), at(y, x - 1, z), at(y + 1, x, z), at(y - 1, x, z)

    barrier = pltpu.get_barrier_semaphore()
    for k in range(1, 4):
        q = lax.rem(p + k, 4)
        pl.semaphore_signal(barrier, inc=1, device_id={"prompt": q}, device_id_type=MESH)
        pl.semaphore_signal(barrier, inc=1, device_id={"prompt": q, "resp": partner}, device_id_type=MESH)
    for d in (partner, xp, xm, yp, ym):
        pl.semaphore_signal(barrier, inc=1, device_id={"resp": d}, device_id_type=MESH)
    for k in range(1, 8):
        for d in (ring(k), ring(-k)):
            pl.semaphore_signal(barrier, inc=1, device_id={"resp": d}, device_id_type=MESH)

    l_q = pltpu.make_async_copy(q_hbm, q_s, local.at[0])
    l_kv = pltpu.make_async_copy(kv_hbm, rbuf.at[0], local.at[1])
    l_seg = pltpu.make_async_copy(seg_hbm, sbuf.at[0], local.at[2])
    l_tile = pltpu.make_async_copy(tiles_hbm.at[p], pbuf.at[r, pl.ds(pl.multiple_of(p * 8, 8), 8)], local.at[3])
    l_tile.start()
    l_kv.start()
    l_seg.start()
    l_q.start()
    l_kv.wait()
    pl.semaphore_wait(barrier, 25)

    counter = [0]
    started = []

    def copy(src, dst, to, when=None, recv_as=None):
        i = counter[0]
        counter[0] += 1
        assert i < NCOPY
        c = pltpu.make_async_remote_copy(
            src_ref=src, dst_ref=dst, send_sem=send.at[i], recv_sem=recv.at[i if recv_as is None else recv_as],
            device_id=to, device_id_type=MESH,
        )
        started.append((c, when))
        c_index[id(c)] = i
        return c

    c_index = {}

    def rs(d):
        return {"resp": d}

    def start(*cs, when=None):
        def go():
            for c in cs:
                c.start()
        if when is None:
            go()
        else:
            pl.when(when)(go)

    waited = set()

    def got(*cs):
        for c in cs:
            if id(c) not in waited:
                waited.add(id(c))
                c.wait_recv()

    halves = (pl.ds(0, 64), pl.ds(64, 64))
    OWN, ROWB = 0, 8
    def tile_at():
        return pbuf.at[r, pl.ds(pl.multiple_of(p * 8, 8), 8)]

    p0 = []
    for k in range(1, 4):
        q = lax.rem(p + k, 4)
        p0.append(copy(tiles_hbm.at[q], tile_at(), {"prompt": q}))
        p0.append(copy(tiles_hbm.at[q], tile_at(), {"prompt": q, "resp": partner}))
    p0.append(copy(tiles_hbm.at[p], tile_at(), rs(partner)))
    segs = [copy(seg_hbm, sbuf.at[k], rs(ring(k))) for k in range(1, 8)]
    src1 = jnp.where(x == 3, ROWB, OWN)
    src3 = jnp.where(x == 0, OWN, ROWB)
    src7 = jnp.where(z == 0, OWN, ROWB)
    tt = [copy(rbuf.at[OWN, h], rbuf.at[ROWB, h], rs(yp)) for h in halves]
    n1 = [copy(rbuf.at[src1, h], rbuf.at[1, h], rs(xp)) for h in halves]
    n3 = [copy(rbuf.at[src3, h], rbuf.at[3, h], rs(xm)) for h in halves]
    xx = [copy(rbuf.at[src7, h], rbuf.at[7, h], rs(partner)) for h in halves]
    m1 = [copy(rbuf.at[1, h], rbuf.at[4, h], rs(partner)) for h in halves]
    m3 = [copy(rbuf.at[3, h], rbuf.at[6, h], rs(partner)) for h in halves]
    lo, hi = halves
    n2 = [
        copy(rbuf.at[1, lo], rbuf.at[2, lo], rs(xp), when=x < 3),
        copy(rbuf.at[3, hi], rbuf.at[2, hi], rs(xm), when=x > 0),
    ]
    n2x = [
        copy(rbuf.at[3, lo], rbuf.at[2, lo], rs(xm), when=x == 1, recv_as=c_index[id(n2[0])]),
        copy(rbuf.at[1, hi], rbuf.at[2, hi], rs(xp), when=x == 2, recv_as=c_index[id(n2[1])]),
    ]
    m2 = [
        copy(rbuf.at[4, lo], rbuf.at[5, lo], rs(xp), when=x < 3),
        copy(rbuf.at[2, hi], rbuf.at[5, hi], rs(partner)),
    ]
    m2x = copy(rbuf.at[6, lo], rbuf.at[5, lo], rs(xm), when=x == 1, recv_as=c_index[id(m2[0])])

    def pair(yy, xx_):
        return pbuf.at[pl.ds(at(yy, xx_, 0), 2)]

    def one(yy, xx_, zz):
        return pbuf.at[at(yy, xx_, zz)]

    pxa = copy(pair(y, x), pair(y, x), rs(xp))
    pxb = copy(pair(y, x), pair(y, x), rs(xm))
    pxc = copy(one(y, x - 1, 0), one(y, x - 1, 0), rs(xp))
    pxd = copy(one(y, x + 1, 1), one(y, x + 1, 1), rs(xm))
    offs = (0, -1, 1, 2)
    pya = [copy(pair(y, x + o), pair(y, x + o), rs(yp)) for o in offs]
    pyb = [copy(pair(y, x + o), pair(y, x + o), rs(ym)) for o in offs]
    pyc = [
        copy(pair(y - 1, x), pair(y - 1, x), rs(yp)),
        copy(one(y - 1, x + 1, 0), one(y - 1, x + 1, 0), rs(yp)),
    ]
    pyd = [
        copy(one(y + 1, x + 1, 1), one(y + 1, x + 1, 1), rs(ym)),
        copy(pair(y + 1, x - 1), pair(y + 1, x - 1), rs(ym)),
        copy(pair(y + 1, x + 2), pair(y + 1, x + 2), rs(ym)),
    ]

    start(*p0, *tt)
    start(n1[0], when=x < 3)
    start(n3[0], when=x == 0)
    start(*xx, when=z == 0)
    start(*segs)
    l_tile.wait()
    got(*p0)
    start(pxa, pxb, pyb[0], pya[0])
    start(n1[1], when=x < 3)
    start(n3[1], when=x == 0)
    l_seg.wait()
    l_q.wait()

    def got_if(cond, c):
        waited.add(id(c))
        pl.when(cond)(c.wait_recv)

    def relay_t(i):
        got(tt[i])
        start(n1[i], when=x == 3)
        start(n3[i], when=x > 0)
        start(xx[i], when=z == 1)

    def relay_pa():
        got(pxa)
        start(pxc, pyb[1], pya[1])

    def relay_pb():
        got(pxb)
        start(pxd, pyb[2], pya[2])

    def relay_pc():
        got(pxc, pxd)
        start(pyb[3], pya[3])

    def take_n1(i, cond):
        got_if(cond, n1[i])
        start(m1[i], when=cond)

    late = set()

    def late_n1(i):
        if i not in late:
            late.add(i)
            take_n1(i, x == 0)
            if i == 0:
                start(n2[0], when=x == 0)

    def send_n2(i):
        if i == 0:
            start(n2[0], when=x < 3)
        else:
            start(n2x[1], when=x == 2)

    def relay_n3(i):
        got(n3[i])
        if i == 0:
            start(n2x[0], when=x == 1)
        else:
            start(n2[1], when=x > 0)
        start(m3[i])

    def relay_m1():
        got(m1[0])
        start(m2[0], when=x < 3)

    def relay_m3():
        got(m3[0])
        start(m2x, when=x == 1)

    def relay_n2():
        got(n2[1])
        start(m2[1])

    def relay_ya(i):
        got(pya[i])
        if i == 0:
            start(pyc[0])
        if i == 2:
            start(pyc[1])

    def relay_yb(i):
        got(pyb[i])
        if i == 2:
            start(pyd[0])
        if i == 1:
            start(pyd[1])
        if i == 3:
            start(pyd[2])

    relays = [
        (11.5, lambda: relay_t(0)),
        (12, lambda: take_n1(0, x > 0)),
        (17, lambda: relay_pb()),
        (17.2, lambda: relay_pa()),
        (17.5, lambda: relay_t(1)),
        (17.6, lambda: pl.when(x > 0)(lambda: send_n2(0))),
        (22, lambda: relay_n3(0)),
        (22.6, lambda: late_n1(0)),
        (23, lambda: relay_ya(0)),
        (24, lambda: take_n1(1, x > 0)),
        (25.8, lambda: relay_pc()),
        (25.9, lambda: send_n2(1)),
        (26, lambda: relay_yb(2)),
        (29, lambda: relay_ya(2)),
        (29.5, lambda: late_n1(1)),
        (31, lambda: relay_m1()),
        (31.5, lambda: relay_n3(1)),
        (32, lambda: relay_yb(1)),
        (37.5, lambda: relay_yb(3)),
        (38, lambda: relay_n2()),
        (38.5, lambda: relay_m3()),
    ]

    def due(t):
        fns = []
        while relays and relays[0][0] <= t:
            fns.append(relays.pop(0)[1])
        return fns

    def relay_until(t):
        for f in due(t):
            f()

    seg_own = jnp.transpose(jnp.broadcast_to(sbuf[0, 0:1].astype(jnp.float32), (128, 128)))
    row = lax.broadcasted_iota(jnp.int32, (128, 128), 0)
    col = lax.broadcasted_iota(jnp.int32, (128, 128), 1)

    def resp_bias(slots):
        for j, s in slots:
            if s == 0:
                d = jnp.int32(0)
            elif s <= 3:
                d = jnp.int32(2 * s)
            elif s <= 6:
                d = 2 * (s - 3) - 1 + 2 * z
            else:
                d = 7 - 6 * z
            theirs = sbuf[d, 0:1].astype(jnp.float32)
            theirs = jnp.where(r >= d, theirs, -1.0)
            ok = seg_own == theirs
            if s == 0:
                ok = ok & (col <= row)
            bias_s[:, j * 128:(j + 1) * 128] = jnp.where(ok, 0.0, NEG)

    def tiles_of(yy, part, lanes):
        xs = ((x, x - 1), (x + 1, x + 2))[part]
        return jnp.concatenate([pbuf[pl.ds(at(yy, c, 0), 2), :, lanes].reshape(64, 128) for c in xs], axis=0)

    def prefix_bias(halves_):
        limit = len_ref[0]
        hot = jnp.where(lax.broadcasted_iota(jnp.int32, (8, 128), 1) == 0, 1.0, 0.0).astype(jnp.bfloat16)
        for j, (yy, part) in halves_:
            marks = tiles_of(yy, part, pl.ds(WIDE, 128))
            places = lax.dot_general(hot, marks, (((1,), (1,)), ((), ())), preferred_element_type=jnp.float32)
            tok = lax.rem(lax.broadcasted_iota(jnp.int32, (1, 128), 1), 8)
            pos = places[0:1].astype(jnp.int32) * 8 + tok
            bias_s[:, j * 128:(j + 1) * 128] = jnp.broadcast_to(jnp.where(pos < limit, 0.0, NEG), (128, 128))

    def resp_cols(slots):
        def load(off):
            return jnp.concatenate([rbuf[s, :, pl.ds(off, 128)] for s in slots], axis=0)
        return load

    def prefix_cols(halves_):
        def load(off):
            return jnp.concatenate([tiles_of(yy, part, pl.ds(off, 128)) for yy, part in halves_], axis=0)
        return load

    nt = (((1,), (1,)), ((), ()))
    nn = (((1,), (0,)), ((), ()))

    def attend(load, width, first, last, t0, dt):
        hooks = [(i, due(t0 + i * dt)) for i in range(KVH)]
        hooks = [(i, fns) for i, fns in hooks if fns]

        def step(h, carry):
            for i, fns in hooks:
                def run(fns=fns):
                    for f in fns:
                        f()
                pl.when(h == i)(run)
            off = pl.multiple_of(h * 128, 128)
            k = load(off)
            v = load(pl.multiple_of(off + KVH * HD, 128))
            bias = bias_s[:, :width * 128]
            for g0 in range(0, 8, G):
                def cols(g):
                    return pl.ds(pl.multiple_of(off * 8 + (g0 + g) * 128, 128), 128)
                qs = jnp.concatenate([q_s[:, cols(g)] for g in range(G)], axis=0)
                scores = lax.dot_general(qs, k, nt, preferred_element_type=jnp.float32)
                ps, als, lss = [], [], []
                for g in range(G):
                    n = h * 8 + g0 + g
                    s = scores[g * 128:(g + 1) * 128] + bias
                    parts = [s[:, j * 128:(j + 1) * 128] for j in range(width)]
                    mx = jnp.max(functools.reduce(jnp.maximum, parts), axis=1, keepdims=True)
                    if first:
                        m = jnp.broadcast_to(mx, (128, 128))
                    else:
                        mo = m_s[n]
                        m = jnp.maximum(mo, mx)
                        al = jnp.exp2((mo - m) * C)
                        als.append(al)
                    w = [jnp.exp2((t - m) * C) for t in parts]
                    ls = functools.reduce(lambda a, b: a + b, w)
                    if not first:
                        ls = ls + l_s[n] * al
                    lss.append(ls)
                    if not last:
                        m_s[n] = m
                        l_s[n] = ls
                    ps.append(jnp.concatenate([t.astype(jnp.bfloat16) for t in w], axis=1))
                pv_all = lax.dot_general(jnp.concatenate(ps, axis=0), v, nn, preferred_element_type=jnp.float32)
                for g in range(G):
                    n = h * 8 + g0 + g
                    pv = pv_all[g * 128:(g + 1) * 128]
                    if not first:
                        pv = pv + acc_s[n] * als[g]
                    if not last:
                        acc_s[n] = pv
                    else:
                        tot = jnp.sum(lss[g], axis=1, keepdims=True)
                        o_s[:, cols(g)] = (pv / tot).astype(jnp.bfloat16)
            return carry
        lax.fori_loop(0, KVH, step, 0)

    def both(slots, halves_):
        loads = [resp_cols(slots)] if slots else []
        loads += [prefix_cols(halves_)] if halves_ else []
        def load(off):
            return jnp.concatenate([f(off) for f in loads], axis=0) if len(loads) > 1 else loads[0](off)
        resp_bias(list(enumerate(slots)))
        prefix_bias([(len(slots) + i, half) for i, half in enumerate(halves_)])
        return load, len(slots) + len(halves_)

    ready = {0: (), 1: n1, 2: n2, 3: n3, 4: m1, 5: m2, 6: m3, 7: xx}

    def need(slots, halves_):
        for s in slots:
            if s == 1:
                late_n1(0)
                late_n1(1)
            got(*ready[s])
        if any(slots):
            got(*segs)
        for d, part in halves_:
            if d == 0:
                got(*((pxa,), (pxb, pxc, pxd))[part])
            elif d == -1:
                got(*((pya[0], pya[1]), (pya[2], pya[3]))[part])
            elif d == 1:
                got(*((pyb[0], pyb[1]), (pyb[2], pyb[3]))[part])
            else:
                got(*((pyc[0], pyd[1]), (pyc[1], pyd[0], pyd[2]))[part])

    def chunk(t0, dt, slots, halves_, first=False, last=False):
        relay_until(t0)
        need(slots, halves_)
        load, width = both(slots, [(y + d, part) for d, part in halves_])
        attend(load, width, first, last, t0, dt)

    chunk(10, 0.4, (0,), (), first=True)
    chunk(18, 0.6, (), ((0, 0),))
    chunk(27, 0.85, (1, 7), ((0, 1), (1, 0)))
    chunk(35, 0.95, (3, 4), ((-1, 0),))
    chunk(42, 0.9, (2,), ((1, 1), (-1, 1)))
    relay_until(100)
    chunk(50, 0.9, (6, 5), ((2, 0), (2, 1)), last=True)
    done = pltpu.make_async_copy(o_s, out_hbm, local.at[4])
    done.start()
    for c, when in started:
        if when is None:
            c.wait_send()
        else:
            pl.when(when)(c.wait_send)
    done.wait()


def on_device(queries, resp_kv, resp_segments, prefix_kv, tile_plan, prompt_lengths):
    tiles, seg8 = sort_tiles(tile_plan.T, prefix_kv, resp_segments)
    anywhere = pl.BlockSpec(memory_space=pl.ANY)
    out = pl.pallas_call(
        main_kernel,
        out_shape=jax.ShapeDtypeStruct((ROWS, H * HD), jnp.bfloat16),
        in_specs=[pl.BlockSpec(memory_space=pltpu.SMEM)] + [anywhere] * 4,
        out_specs=anywhere,
        scratch_shapes=[
            VMEM((ROWS, H * HD), jnp.bfloat16),
            VMEM((9, ROWS, WIDE), jnp.bfloat16),
            VMEM((8, 8, 128), jnp.int32),
            VMEM((32, 32, PWIDE), jnp.bfloat16),
            VMEM((H, ROWS, 128), jnp.float32),
            VMEM((H, ROWS, 128), jnp.float32),
            VMEM((H, ROWS, 128), jnp.float32),
            VMEM((ROWS, 640), jnp.float32),
            VMEM((ROWS, H * HD), jnp.bfloat16),
            pltpu.SemaphoreType.DMA((NCOPY,)),
            pltpu.SemaphoreType.DMA((NCOPY,)),
            pltpu.SemaphoreType.DMA((5,)),
        ],
        compiler_params=pltpu.CompilerParams(
            collective_id=0, has_side_effects=True, vmem_limit_bytes=60 << 20
        ),
        name="attend",
    )(prompt_lengths, queries[0], resp_kv[0], seg8, tiles)
    return out[None]


def solution(mesh):
    return jax.shard_map(
        on_device,
        mesh=mesh,
        in_specs=(
            P("prompt", "resp", None),
            P("prompt", "resp", None),
            P("prompt", "resp"),
            P(("prompt", "resp"), None, None),
            P(("prompt", "resp"), None),
            P("prompt"),
        ),
        out_specs=P("prompt", "resp", None),
        check_vma=False,
    )
```

```python
import functools
import math

import jax
import jax.numpy as jnp
from jax import lax
from jax.experimental import pallas as pl
from jax.experimental.pallas import tpu as pltpu
from jax.sharding import PartitionSpec as P

H = 64
KVH = 8
HD = 128
ROWS = 128
TILE = 8
WIDE = 2 * KVH * HD
PWIDE = WIDE + 128
NEG = -1e30
C = math.log2(math.e) / math.sqrt(HD)
MESH = pl.DeviceIdType.MESH
VMEM = pltpu.VMEM
G = 8


NCOPY = 64


def main_kernel(
    len_ref, plan_ref, q_hbm, kv_hbm, seg_hbm, prefix_hbm, o_s,
    q_s, raw, tiles, rbuf, sbuf, pbuf, m_s, l_s, acc_s, bias_s,
    send, recv, local,
):
    p = lax.axis_index("prompt")
    r = lax.axis_index("resp")
    z = lax.rem(r, 2)
    x = lax.rem(r // 2, 4)
    y = r // 8

    def at(yy, xx, zz):
        return lax.rem(yy + 4, 4) * 8 + lax.rem(xx + 4, 4) * 2 + zz

    def ring(d):
        return lax.rem(r + 32 + d, 32)

    partner = r + 1 - 2 * z
    xp, xm, yp, ym = at(y, x + 1, z), at(y, x - 1, z), at(y + 1, x, z), at(y - 1, x, z)

    l_raw = pltpu.make_async_copy(prefix_hbm, raw, local.at[4])
    l_raw.start()
    barrier = pltpu.get_barrier_semaphore()
    for k in range(1, 4):
        q = lax.rem(p + k, 4)
        pl.semaphore_signal(barrier, inc=1, device_id={"prompt": q}, device_id_type=MESH)
        pl.semaphore_signal(barrier, inc=1, device_id={"prompt": q, "resp": partner}, device_id_type=MESH)
    for d in (partner, xp, xm, yp, ym):
        pl.semaphore_signal(barrier, inc=1, device_id={"resp": d}, device_id_type=MESH)
    for k in range(1, 8):
        for d in (ring(k), ring(-k)):
            pl.semaphore_signal(barrier, inc=1, device_id={"resp": d}, device_id_type=MESH)

    l_q = pltpu.make_async_copy(q_hbm, q_s, local.at[0])
    l_kv = pltpu.make_async_copy(kv_hbm, rbuf.at[0], local.at[1])
    l_seg = pltpu.make_async_copy(seg_hbm, sbuf.at[0], local.at[2])
    l_tile = pltpu.make_async_copy(tiles.at[p], pbuf.at[r, pl.ds(pl.multiple_of(p * 8, 8), 8)], local.at[3])
    l_kv.start()
    l_seg.start()
    l_q.start()
    l_raw.wait()
    for q in range(4):
        slot = jnp.int32(0)
        place = jnp.int32(0)
        for t in range(4):
            hit = plan_ref[0, t] == q
            slot = jnp.where(hit, t, slot)
            place = jnp.where(hit, plan_ref[1, t], place)
        tiles[q, :, :WIDE] = raw[slot]
        tiles[q, :, WIDE:] = jnp.full((TILE, 128), place, jnp.int32).astype(jnp.float32).astype(jnp.bfloat16)
    l_kv.wait()
    pl.semaphore_wait(barrier, 25)
    l_tile.start()

    counter = [0]
    started = []

    def copy(src, dst, to, when=None, recv_as=None):
        i = counter[0]
        counter[0] += 1
        assert i < NCOPY
        c = pltpu.make_async_remote_copy(
            src_ref=src, dst_ref=dst, send_sem=send.at[i], recv_sem=recv.at[i if recv_as is None else recv_as],
            device_id=to, device_id_type=MESH,
        )
        started.append((c, when))
        c_index[id(c)] = i
        return c

    c_index = {}

    def rs(d):
        return {"resp": d}

    def start(*cs, when=None):
        def go():
            for c in cs:
                c.start()
        if when is None:
            go()
        else:
            pl.when(when)(go)

    waited = set()

    def got(*cs):
        for c in cs:
            if id(c) not in waited:
                waited.add(id(c))
                c.wait_recv()

    halves = (pl.ds(0, 64), pl.ds(64, 64))
    OWN, ROWB = 0, 8
    def tile_at():
        return pbuf.at[r, pl.ds(pl.multiple_of(p * 8, 8), 8)]

    p0 = []
    for k in range(1, 4):
        q = lax.rem(p + k, 4)
        p0.append(copy(tiles.at[q], tile_at(), {"prompt": q}))
        p0.append(copy(tiles.at[q], tile_at(), {"prompt": q, "resp": partner}))
    p0.append(copy(tiles.at[p], tile_at(), rs(partner)))
    segs = [copy(seg_hbm, sbuf.at[k], rs(ring(k))) for k in range(1, 8)]
    src1 = jnp.where(x == 3, ROWB, OWN)
    src3 = jnp.where(x == 0, OWN, ROWB)
    src7 = jnp.where(z == 0, OWN, ROWB)
    tt = [copy(rbuf.at[OWN, h], rbuf.at[ROWB, h], rs(yp)) for h in halves]
    n1 = [copy(rbuf.at[src1, h], rbuf.at[1, h], rs(xp)) for h in halves]
    n3 = [copy(rbuf.at[src3, h], rbuf.at[3, h], rs(xm)) for h in halves]
    xx = [copy(rbuf.at[src7, h], rbuf.at[7, h], rs(partner)) for h in halves]
    m1 = [copy(rbuf.at[1, h], rbuf.at[4, h], rs(partner)) for h in halves]
    m3 = [copy(rbuf.at[3, h], rbuf.at[6, h], rs(partner)) for h in halves]
    lo, hi = halves
    n2 = [
        copy(rbuf.at[1, lo], rbuf.at[2, lo], rs(xp), when=x < 3),
        copy(rbuf.at[3, hi], rbuf.at[2, hi], rs(xm), when=x > 0),
    ]
    n2x = [
        copy(rbuf.at[3, lo], rbuf.at[2, lo], rs(xm), when=x == 1, recv_as=c_index[id(n2[0])]),
        copy(rbuf.at[1, hi], rbuf.at[2, hi], rs(xp), when=x == 2, recv_as=c_index[id(n2[1])]),
    ]
    m2 = [
        copy(rbuf.at[4, lo], rbuf.at[5, lo], rs(xp), when=x < 3),
        copy(rbuf.at[2, hi], rbuf.at[5, hi], rs(partner)),
    ]
    m2x = copy(rbuf.at[6, lo], rbuf.at[5, lo], rs(xm), when=x == 1, recv_as=c_index[id(m2[0])])

    def pair(yy, xx_):
        return pbuf.at[pl.ds(at(yy, xx_, 0), 2)]

    def one(yy, xx_, zz):
        return pbuf.at[at(yy, xx_, zz)]

    pxa = copy(pair(y, x), pair(y, x), rs(xp))
    pxb = copy(pair(y, x), pair(y, x), rs(xm))
    pxc = copy(one(y, x - 1, 0), one(y, x - 1, 0), rs(xp))
    pxd = copy(one(y, x + 1, 1), one(y, x + 1, 1), rs(xm))
    offs = (0, -1, 1, 2)
    pya = [copy(pair(y, x + o), pair(y, x + o), rs(yp)) for o in offs]
    pyb = [copy(pair(y, x + o), pair(y, x + o), rs(ym)) for o in offs]
    pyc = [
        copy(pair(y - 1, x), pair(y - 1, x), rs(yp)),
        copy(one(y - 1, x + 1, 0), one(y - 1, x + 1, 0), rs(yp)),
    ]
    pyd = [
        copy(one(y + 1, x + 1, 1), one(y + 1, x + 1, 1), rs(ym)),
        copy(pair(y + 1, x - 1), pair(y + 1, x - 1), rs(ym)),
        copy(pair(y + 1, x + 2), pair(y + 1, x + 2), rs(ym)),
    ]

    start(*p0, *tt)
    start(n1[0], when=x < 3)
    start(n3[0], when=x == 0)
    start(*xx, when=z == 0)
    start(*segs)
    l_tile.wait()
    got(*p0)
    start(pxa, pxb, pyb[0], pya[0])
    start(n1[1], when=x < 3)
    start(n3[1], when=x == 0)
    l_seg.wait()
    l_q.wait()

    def got_if(cond, c):
        waited.add(id(c))
        pl.when(cond)(c.wait_recv)

    def relay_t(i):
        got(tt[i])
        start(n1[i], when=x == 3)
        start(n3[i], when=x > 0)
        start(xx[i], when=z == 1)

    def relay_pa():
        got(pxa)
        start(pxc, pyb[1], pya[1])

    def relay_pb():
        got(pxb)
        start(pxd, pyb[2], pya[2])

    def relay_pc():
        got(pxc, pxd)
        start(pyb[3], pya[3])

    def take_n1(i, cond):
        got_if(cond, n1[i])
        start(m1[i], when=cond)

    late = set()

    def late_n1(i):
        if i not in late:
            late.add(i)
            take_n1(i, x == 0)
            if i == 0:
                start(n2[0], when=x == 0)

    def send_n2(i):
        if i == 0:
            start(n2[0], when=x < 3)
        else:
            start(n2x[1], when=x == 2)

    def relay_n3(i):
        got(n3[i])
        if i == 0:
            start(n2x[0], when=x == 1)
        else:
            start(n2[1], when=x > 0)
        start(m3[i])

    def relay_m1(cond):
        got_if(cond, m1[0])
        start(m2[0], when=cond & (x < 3))

    def relay_m3():
        got(m3[0])
        start(m2x, when=x == 1)

    def relay_n2():
        got(n2[1])
        start(m2[1])

    def relay_ya(i):
        got(pya[i])
        if i == 0:
            start(pyc[0])
        if i == 2:
            start(pyc[1])

    def relay_yb(i):
        got(pyb[i])
        if i == 2:
            start(pyd[0])
        if i == 1:
            start(pyd[1])
        if i == 3:
            start(pyd[2])

    relays = [
        (11.5, lambda: relay_t(0)),
        (12, lambda: take_n1(0, x > 0)),
        (17, lambda: relay_pb()),
        (17.2, lambda: relay_pa()),
        (17.5, lambda: relay_t(1)),
        (17.6, lambda: pl.when(x > 0)(lambda: send_n2(0))),
        (22, lambda: relay_n3(0)),
        (22.6, lambda: late_n1(0)),
        (23, lambda: relay_ya(0)),
        (24, lambda: take_n1(1, x > 0)),
        (25.8, lambda: relay_pc()),
        (25.9, lambda: send_n2(1)),
        (26, lambda: relay_yb(2)),
        (29, lambda: relay_ya(2)),
                (31.2, lambda: relay_n3(1)),
        (31.4, lambda: relay_m1(x > 0)),
        (32, lambda: relay_yb(1)),
        (33.5, lambda: late_n1(1)),
        (37.5, lambda: relay_yb(3)),
        (38, lambda: relay_n2()),
        (38.5, lambda: relay_m3()),
        (41, lambda: relay_m1(x == 0)),
    ]

    def due(t):
        fns = []
        while relays and relays[0][0] <= t:
            fns.append(relays.pop(0)[1])
        return fns

    def relay_until(t):
        for f in due(t):
            f()

    seg_own = jnp.transpose(jnp.broadcast_to(sbuf[0].astype(jnp.float32), (128, 128)))
    row = lax.broadcasted_iota(jnp.int32, (128, 128), 0)
    col = lax.broadcasted_iota(jnp.int32, (128, 128), 1)

    def resp_bias(slots):
        for j, s in slots:
            if s == 0:
                d = jnp.int32(0)
            elif s <= 3:
                d = jnp.int32(2 * s)
            elif s <= 6:
                d = 2 * (s - 3) - 1 + 2 * z
            else:
                d = 7 - 6 * z
            theirs = sbuf[d].astype(jnp.float32)
            theirs = jnp.where(r >= d, theirs, -1.0)
            ok = seg_own == theirs
            if s == 0:
                ok = ok & (col <= row)
            bias_s[:, j * 128:(j + 1) * 128] = jnp.where(ok, 0.0, NEG)

    def tiles_of(yy, part, lanes):
        xs = ((x, x - 1), (x + 1, x + 2))[part]
        return jnp.concatenate([pbuf[pl.ds(at(yy, c, 0), 2), :, lanes].reshape(64, 128) for c in xs], axis=0)

    def prefix_bias(halves_):
        limit = len_ref[0]
        hot = jnp.where(lax.broadcasted_iota(jnp.int32, (8, 128), 1) == 0, 1.0, 0.0).astype(jnp.bfloat16)
        for j, (yy, part) in halves_:
            marks = tiles_of(yy, part, pl.ds(WIDE, 128))
            places = lax.dot_general(hot, marks, (((1,), (1,)), ((), ())), preferred_element_type=jnp.float32)
            tok = lax.rem(lax.broadcasted_iota(jnp.int32, (1, 128), 1), 8)
            pos = places[0:1].astype(jnp.int32) * 8 + tok
            bias_s[:, j * 128:(j + 1) * 128] = jnp.broadcast_to(jnp.where(pos < limit, 0.0, NEG), (128, 128))

    def resp_cols(slots):
        def load(off):
            return jnp.concatenate([rbuf[s, :, pl.ds(off, 128)] for s in slots], axis=0)
        return load

    def prefix_cols(halves_):
        def load(off):
            return jnp.concatenate([tiles_of(yy, part, pl.ds(off, 128)) for yy, part in halves_], axis=0)
        return load

    nt = (((1,), (1,)), ((), ()))
    nn = (((1,), (0,)), ((), ()))

    def attend(load, width, first, last, t0, dt):
        hooks = [(i, due(t0 + 2 * i * dt)) for i in range(KVH // 2)]
        hooks = [(i, fns) for i, fns in hooks if fns]

        def step(i, carry):
            for j, fns in hooks:
                def run(fns=fns):
                    for f in fns:
                        f()
                pl.when(i == j)(run)
            head(2 * i)
            head(2 * i + 1)
            return carry

        def head(h):
            off = pl.multiple_of(h * 128, 128)
            k = load(off)
            v = load(pl.multiple_of(off + KVH * HD, 128))
            bias = bias_s[:, :width * 128]
            for g0 in range(0, 8, G):
                def cols(g):
                    return pl.ds(pl.multiple_of(off * 8 + (g0 + g) * 128, 128), 128)
                qs = jnp.concatenate([q_s[:, cols(g)] for g in range(G)], axis=0)
                scores = lax.dot_general(qs, k, nt, preferred_element_type=jnp.float32)
                ps, als, lss = [], [], []
                for g in range(G):
                    n = h * 8 + g0 + g
                    s = scores[g * 128:(g + 1) * 128] + bias
                    parts = [s[:, j * 128:(j + 1) * 128] for j in range(width)]
                    mx = jnp.max(functools.reduce(jnp.maximum, parts), axis=1, keepdims=True)
                    if first:
                        m = jnp.broadcast_to(mx, (128, 128))
                    else:
                        mo = m_s[n]
                        m = jnp.maximum(mo, mx)
                        al = jnp.exp2((mo - m) * C)
                        als.append(al)
                    w = [jnp.exp2((t - m) * C) for t in parts]
                    ls = functools.reduce(lambda a, b: a + b, w)
                    if not first:
                        ls = ls + l_s[n] * al
                    lss.append(ls)
                    if not last:
                        m_s[n] = m
                        l_s[n] = ls
                    ps.append(jnp.concatenate([t.astype(jnp.bfloat16) for t in w], axis=1))
                pv_all = lax.dot_general(jnp.concatenate(ps, axis=0), v, nn, preferred_element_type=jnp.float32)
                for g in range(G):
                    n = h * 8 + g0 + g
                    pv = pv_all[g * 128:(g + 1) * 128]
                    if not first:
                        pv = pv + acc_s[n] * als[g]
                    if not last:
                        acc_s[n] = pv
                    else:
                        tot = jnp.sum(lss[g], axis=1, keepdims=True)
                        o_s[:, cols(g)] = (pv / tot).astype(jnp.bfloat16)

        lax.fori_loop(0, KVH // 2, step, 0)

    def both(slots, halves_):
        loads = [resp_cols(slots)] if slots else []
        loads += [prefix_cols(halves_)] if halves_ else []
        def load(off):
            return jnp.concatenate([f(off) for f in loads], axis=0) if len(loads) > 1 else loads[0](off)
        resp_bias(list(enumerate(slots)))
        prefix_bias([(len(slots) + i, half) for i, half in enumerate(halves_)])
        return load, len(slots) + len(halves_)

    ready = {0: (), 1: n1, 2: n2, 3: n3, 4: m1, 5: m2, 6: m3, 7: xx}

    def need(slots, halves_):
        for s in slots:
            if s == 1:
                late_n1(0)
                late_n1(1)
            if s == 4:
                relay_until(41)
            got(*ready[s])
        if any(slots):
            got(*segs)
        for d, part in halves_:
            if d == 0:
                got(*((pxa,), (pxb, pxc, pxd))[part])
            elif d == -1:
                got(*((pya[0], pya[1]), (pya[2], pya[3]))[part])
            elif d == 1:
                got(*((pyb[0], pyb[1]), (pyb[2], pyb[3]))[part])
            else:
                got(*((pyc[0], pyd[1]), (pyc[1], pyd[0], pyd[2]))[part])

    def chunk(t0, dt, slots, halves_, first=False, last=False):
        relay_until(t0)
        need(slots, halves_)
        load, width = both(slots, [(y + d, part) for d, part in halves_])
        attend(load, width, first, last, t0, dt)

    chunk(10, 0.5, (0,), (), first=True)
    chunk(17.8, 0.5, (), ((0, 0),))
    chunk(27.5, 0.6, (7,), ((0, 1),))
    chunk(32.5, 0.6, (3,), ((1, 0),))
    chunk(37, 0.75, (1,), ((1, 1), (-1, 0)))
    chunk(44, 0.75, (4, 2, 6), ())
    relay_until(100)
    chunk(52, 0.9, (5,), ((-1, 1), (2, 0), (2, 1)), last=True)
    for c, when in started:
        if when is None:
            c.wait_send()
        else:
            pl.when(when)(c.wait_send)


def on_device(queries, resp_kv, resp_segments, prefix_kv, tile_plan, prompt_lengths):
    anywhere = pl.BlockSpec(memory_space=pl.ANY)
    inside = pl.BlockSpec(memory_space=VMEM)
    out = pl.pallas_call(
        main_kernel,
        out_shape=jax.ShapeDtypeStruct((ROWS, H * HD), jnp.bfloat16),
        in_specs=[pl.BlockSpec(memory_space=pltpu.SMEM)] * 2 + [anywhere] * 4,
        out_specs=inside,
        scratch_shapes=[
            VMEM((ROWS, H * HD), jnp.bfloat16),
            VMEM((4, TILE, WIDE), jnp.bfloat16),
            VMEM((4, TILE, PWIDE), jnp.bfloat16),
            VMEM((9, ROWS, WIDE), jnp.bfloat16),
            VMEM((8, 1, 128), jnp.int32),
            VMEM((32, 32, PWIDE), jnp.bfloat16),
            VMEM((H, ROWS, 128), jnp.float32),
            VMEM((H, ROWS, 128), jnp.float32),
            VMEM((H, ROWS, 128), jnp.float32),
            VMEM((ROWS, 640), jnp.float32),
            pltpu.SemaphoreType.DMA((NCOPY,)),
            pltpu.SemaphoreType.DMA((NCOPY,)),
            pltpu.SemaphoreType.DMA((5,)),
        ],
        compiler_params=pltpu.CompilerParams(
            collective_id=0, has_side_effects=True, vmem_limit_bytes=40 << 20
        ),
        name="attend",
    )(prompt_lengths, tile_plan.T, *(pltpu.with_memory_space_constraint(t, pltpu.HBM) for t in (queries[0], resp_kv[0], resp_segments, prefix_kv)))
    return out[None]


def solution(mesh):
    return jax.shard_map(
        on_device,
        mesh=mesh,
        in_specs=(
            P("prompt", "resp", None),
            P("prompt", "resp", None),
            P("prompt", "resp"),
            P(("prompt", "resp"), None, None),
            P(("prompt", "resp"), None),
            P("prompt"),
        ),
        out_specs=P("prompt", "resp", None),
        check_vma=False,
    )
```

```python
import functools
import math

import jax
import jax.numpy as jnp
from jax import lax
from jax.experimental import pallas as pl
from jax.experimental.pallas import tpu as pltpu
from jax.sharding import PartitionSpec as P

H = 64
KVH = 8
HD = 128
ROWS = 128
TILE = 8
WIDE = 2 * KVH * HD
PWIDE = WIDE + 128
NEG = -1e30
C = math.log2(math.e) / math.sqrt(HD)
MESH = pl.DeviceIdType.MESH
VMEM = pltpu.VMEM
G = 8


NCOPY = 64


def main_kernel(
    len_ref, plan_ref, q_hbm, kv_hbm, seg_hbm, prefix_hbm, o_s,
    q_s, raw, tiles, rbuf, sbuf, pbuf, m_s, l_s, acc_s, bias_s, rb_s,
    send, recv, local,
):
    p = lax.axis_index("prompt")
    r = lax.axis_index("resp")
    z = lax.rem(r, 2)
    x = lax.rem(r // 2, 4)
    y = r // 8

    def at(yy, xx, zz):
        return lax.rem(yy + 4, 4) * 8 + lax.rem(xx + 4, 4) * 2 + zz

    def ring(d):
        return lax.rem(r + 32 + d, 32)

    partner = r + 1 - 2 * z
    xp, xm, yp, ym = at(y, x + 1, z), at(y, x - 1, z), at(y + 1, x, z), at(y - 1, x, z)

    l_raw = pltpu.make_async_copy(prefix_hbm, raw, local.at[4])
    l_raw.start()
    barrier = pltpu.get_barrier_semaphore()
    for k in range(1, 4):
        q = lax.rem(p + k, 4)
        pl.semaphore_signal(barrier, inc=1, device_id={"prompt": q}, device_id_type=MESH)
        pl.semaphore_signal(barrier, inc=1, device_id={"prompt": q, "resp": partner}, device_id_type=MESH)
    for d in (partner, xp, xm, yp, ym):
        pl.semaphore_signal(barrier, inc=1, device_id={"resp": d}, device_id_type=MESH)
    for k in range(1, 8):
        for d in (ring(k), ring(-k)):
            pl.semaphore_signal(barrier, inc=1, device_id={"resp": d}, device_id_type=MESH)

    l_q = pltpu.make_async_copy(q_hbm, q_s, local.at[0])
    l_kv = pltpu.make_async_copy(kv_hbm, rbuf.at[0], local.at[1])
    l_seg = pltpu.make_async_copy(seg_hbm, sbuf.at[0], local.at[2])
    l_tile = pltpu.make_async_copy(tiles.at[p], pbuf.at[r, pl.ds(pl.multiple_of(p * 8, 8), 8)], local.at[3])
    l_kv.start()
    l_seg.start()
    l_q.start()
    l_raw.wait()
    for q in range(4):
        slot = jnp.int32(0)
        place = jnp.int32(0)
        for t in range(4):
            hit = plan_ref[0, t] == q
            slot = jnp.where(hit, t, slot)
            place = jnp.where(hit, plan_ref[1, t], place)
        tiles[q, :, :WIDE] = raw[slot]
        tiles[q, :, WIDE:] = jnp.full((TILE, 128), place, jnp.int32).astype(jnp.float32).astype(jnp.bfloat16)
    l_kv.wait()
    pl.semaphore_wait(barrier, 25)
    l_tile.start()

    counter = [0]
    started = []

    def copy(src, dst, to, when=None, recv_as=None):
        i = counter[0]
        counter[0] += 1
        assert i < NCOPY
        c = pltpu.make_async_remote_copy(
            src_ref=src, dst_ref=dst, send_sem=send.at[i], recv_sem=recv.at[i if recv_as is None else recv_as],
            device_id=to, device_id_type=MESH,
        )
        started.append((c, when))
        c_index[id(c)] = i
        return c

    c_index = {}

    def rs(d):
        return {"resp": d}

    def start(*cs, when=None):
        def go():
            for c in cs:
                c.start()
        if when is None:
            go()
        else:
            pl.when(when)(go)

    waited = set()

    def got(*cs):
        for c in cs:
            if id(c) not in waited:
                waited.add(id(c))
                c.wait_recv()

    halves = (pl.ds(0, 64), pl.ds(64, 64))
    OWN, ROWB = 0, 8
    def tile_at():
        return pbuf.at[r, pl.ds(pl.multiple_of(p * 8, 8), 8)]

    p0 = []
    for k in range(1, 4):
        q = lax.rem(p + k, 4)
        p0.append(copy(tiles.at[q], tile_at(), {"prompt": q}))
        p0.append(copy(tiles.at[q], tile_at(), {"prompt": q, "resp": partner}))
    p0.append(copy(tiles.at[p], tile_at(), rs(partner)))
    segs = [copy(seg_hbm, sbuf.at[k], rs(ring(k))) for k in range(1, 8)]
    src1 = jnp.where(x == 3, ROWB, OWN)
    src3 = jnp.where(x == 0, OWN, ROWB)
    src7 = jnp.where(z == 0, OWN, ROWB)
    tt = [copy(rbuf.at[OWN, h], rbuf.at[ROWB, h], rs(yp)) for h in halves]
    n1 = [copy(rbuf.at[src1, h], rbuf.at[1, h], rs(xp)) for h in halves]
    n3 = [copy(rbuf.at[src3, h], rbuf.at[3, h], rs(xm)) for h in halves]
    xx = [copy(rbuf.at[src7, h], rbuf.at[7, h], rs(partner)) for h in halves]
    m1 = [copy(rbuf.at[1, h], rbuf.at[4, h], rs(partner)) for h in halves]
    m3 = [copy(rbuf.at[3, h], rbuf.at[6, h], rs(partner)) for h in halves]
    lo, hi = halves
    n2 = [
        copy(rbuf.at[1, lo], rbuf.at[2, lo], rs(xp), when=x < 3),
        copy(rbuf.at[3, hi], rbuf.at[2, hi], rs(xm), when=x > 0),
    ]
    n2x = [
        copy(rbuf.at[3, lo], rbuf.at[2, lo], rs(xm), when=x == 1, recv_as=c_index[id(n2[0])]),
        copy(rbuf.at[1, hi], rbuf.at[2, hi], rs(xp), when=x == 2, recv_as=c_index[id(n2[1])]),
    ]
    m2 = [
        copy(rbuf.at[4, lo], rbuf.at[5, lo], rs(xp), when=x < 3),
        copy(rbuf.at[2, hi], rbuf.at[5, hi], rs(partner)),
    ]
    m2x = copy(rbuf.at[6, lo], rbuf.at[5, lo], rs(xm), when=x == 1, recv_as=c_index[id(m2[0])])

    def pair(yy, xx_):
        return pbuf.at[pl.ds(at(yy, xx_, 0), 2)]

    def one(yy, xx_, zz):
        return pbuf.at[at(yy, xx_, zz)]

    pxa = copy(pair(y, x), pair(y, x), rs(xp))
    pxb = copy(pair(y, x), pair(y, x), rs(xm))
    pxc = copy(one(y, x - 1, 0), one(y, x - 1, 0), rs(xp))
    pxd = copy(one(y, x + 1, 1), one(y, x + 1, 1), rs(xm))
    offs = (0, -1, 1, 2)
    pya = [copy(pair(y, x + o), pair(y, x + o), rs(yp)) for o in offs]
    pyb = [copy(pair(y, x + o), pair(y, x + o), rs(ym)) for o in offs]
    pyc = [
        copy(pair(y - 1, x), pair(y - 1, x), rs(yp)),
        copy(one(y - 1, x + 1, 0), one(y - 1, x + 1, 0), rs(yp)),
    ]
    pyd = [
        copy(one(y + 1, x + 1, 1), one(y + 1, x + 1, 1), rs(ym)),
        copy(pair(y + 1, x - 1), pair(y + 1, x - 1), rs(ym)),
        copy(pair(y + 1, x + 2), pair(y + 1, x + 2), rs(ym)),
    ]

    start(*p0, *tt)
    start(n1[0], when=x < 3)
    start(n3[0], when=x == 0)
    start(*xx, when=z == 0)
    start(*segs)
    l_tile.wait()
    got(*p0)
    start(pxa, pxb, pyb[0], pya[0])
    start(n1[1], when=x < 3)
    start(n3[1], when=x == 0)
    l_seg.wait()
    l_q.wait()

    def got_if(cond, c):
        waited.add(id(c))
        pl.when(cond)(c.wait_recv)

    def relay_t(i):
        got(tt[i])
        start(n1[i], when=x == 3)
        start(n3[i], when=x > 0)
        start(xx[i], when=z == 1)

    def relay_pa():
        got(pxa)
        start(pxc, pyb[1], pya[1])

    def relay_pb():
        got(pxb)
        start(pxd, pyb[2], pya[2])

    def relay_pc():
        got(pxc, pxd)
        start(pyb[3], pya[3])

    def take_n1(i, cond):
        got_if(cond, n1[i])
        start(m1[i], when=cond)

    late = set()

    def late_n1(i):
        if i not in late:
            late.add(i)
            take_n1(i, x == 0)
            if i == 0:
                start(n2[0], when=x == 0)

    def send_n2(i):
        if i == 0:
            start(n2[0], when=x < 3)
        else:
            start(n2x[1], when=x == 2)

    def relay_n3(i):
        got(n3[i])
        if i == 0:
            start(n2x[0], when=x == 1)
        else:
            start(n2[1], when=x > 0)
        start(m3[i])

    def relay_m1(cond):
        got_if(cond, m1[0])
        start(m2[0], when=cond & (x < 3))

    def relay_m3():
        got(m3[0])
        start(m2x, when=x == 1)

    def relay_n2(cond):
        got_if(cond, n2[1])
        start(m2[1], when=cond)

    def relay_ya(i):
        got(pya[i])
        if i == 0:
            start(pyc[0])
        if i == 2:
            start(pyc[1])

    def relay_yb(i):
        got(pyb[i])
        if i == 2:
            start(pyd[0])
        if i == 1:
            start(pyd[1])
        if i == 3:
            start(pyd[2])

    relays = [
        (11.5, lambda: relay_t(0)),
        (12, lambda: take_n1(0, x > 0)),
        (17, lambda: relay_pb()),
        (17.2, lambda: relay_pa()),
        (17.5, lambda: relay_t(1)),
        (17.6, lambda: pl.when(x > 0)(lambda: send_n2(0))),
        (22, lambda: relay_n3(0)),
        (22.6, lambda: late_n1(0)),
        (23, lambda: relay_ya(0)),
        (24, lambda: take_n1(1, x > 0)),
        (25.8, lambda: relay_pc()),
        (25.9, lambda: send_n2(1)),
        (26, lambda: relay_yb(2)),
        (29, lambda: relay_ya(2)),
                (31.2, lambda: relay_n3(1)),
        (31.4, lambda: relay_m1(x > 0)),
        (32, lambda: relay_yb(1)),
        (33.5, lambda: late_n1(1)),
        (37.5, lambda: relay_yb(3)),
        (38, lambda: relay_n2(x > 0)),
        (38.5, lambda: relay_m3()),
        (41, lambda: relay_m1(x == 0)),
        (43, lambda: relay_n2(x == 0)),
    ]

    def due(t):
        fns = []
        while relays and relays[0][0] <= t:
            fns.append(relays.pop(0)[1])
        return fns

    def relay_until(t):
        for f in due(t):
            f()

    seg_own = jnp.transpose(jnp.broadcast_to(sbuf[0].astype(jnp.float32), (128, 128)))
    row = lax.broadcasted_iota(jnp.int32, (128, 128), 0)
    col = lax.broadcasted_iota(jnp.int32, (128, 128), 1)

    def resp_bias(s):
        if s == 0:
            d = jnp.int32(0)
        elif s <= 3:
            d = jnp.int32(2 * s)
        elif s <= 6:
            d = 2 * (s - 3) - 1 + 2 * z
        else:
            d = 7 - 6 * z
        theirs = sbuf[d].astype(jnp.float32)
        theirs = jnp.where(r >= d, theirs, -1.0)
        ok = seg_own == theirs
        if s == 0:
            ok = ok & (col <= row)
        rb_s[s] = jnp.where(ok, 0.0, NEG)

    def all_resp_bias():
        got(*segs)
        for s in range(1, 8):
            resp_bias(s)

    def tiles_of(yy, part, lanes):
        xs = ((x, x - 1), (x + 1, x + 2))[part]
        return jnp.concatenate([pbuf[pl.ds(at(yy, c, 0), 2), :, lanes].reshape(64, 128) for c in xs], axis=0)

    def prefix_bias(halves_):
        limit = len_ref[0]
        hot = jnp.where(lax.broadcasted_iota(jnp.int32, (8, 128), 1) == 0, 1.0, 0.0).astype(jnp.bfloat16)
        for j, (yy, part) in halves_:
            marks = tiles_of(yy, part, pl.ds(WIDE, 128))
            places = lax.dot_general(hot, marks, (((1,), (1,)), ((), ())), preferred_element_type=jnp.float32)
            tok = lax.rem(lax.broadcasted_iota(jnp.int32, (1, 128), 1), 8)
            pos = places[0:1].astype(jnp.int32) * 8 + tok
            bias_s[:, j * 128:(j + 1) * 128] = jnp.broadcast_to(jnp.where(pos < limit, 0.0, NEG), (8, 128))

    def resp_cols(slots):
        def load(off):
            return jnp.concatenate([rbuf[where_is[s], :, pl.ds(off, 128)] for s in slots], axis=0)
        return load

    def prefix_cols(halves_):
        def load(off):
            return jnp.concatenate([tiles_of(yy, part, pl.ds(off, 128)) for yy, part in halves_], axis=0)
        return load

    nt = (((1,), (1,)), ((), ()))
    nn = (((1,), (0,)), ((), ()))

    def attend(load, bias_of, width, first, last, t0, dt, per):
        hooks = [(i, due(t0 + per * i * dt)) for i in range(KVH // per)]
        hooks = [(i, fns) for i, fns in hooks if fns]

        def step(i, carry):
            for j, fns in hooks:
                def run(fns=fns):
                    for f in fns:
                        f()
                pl.when(i == j)(run)
            for j in range(per):
                head(per * i + j)
            return carry

        def head(h):
            off = pl.multiple_of(h * 128, 128)
            k = load(off)
            v = load(pl.multiple_of(off + KVH * HD, 128))
            bias = bias_of()
            for g0 in range(0, 8, G):
                def cols(g):
                    return pl.ds(pl.multiple_of(off * 8 + (g0 + g) * 128, 128), 128)
                qs = jnp.concatenate([q_s[:, cols(g)] for g in range(G)], axis=0)
                scores = lax.dot_general(qs, k, nt, preferred_element_type=jnp.float32)
                ps, als, lss = [], [], []
                for g in range(G):
                    n = h * 8 + g0 + g
                    s = scores[g * 128:(g + 1) * 128] + bias
                    parts = [s[:, j * 128:(j + 1) * 128] for j in range(width)]
                    mx = jnp.max(functools.reduce(jnp.maximum, parts), axis=1, keepdims=True)
                    if first:
                        m = jnp.broadcast_to(mx, (128, 128))
                    else:
                        mo = m_s[n]
                        m = jnp.maximum(mo, mx)
                        al = jnp.exp2((mo - m) * C)
                        als.append(al)
                    w = [jnp.exp2((t - m) * C) for t in parts]
                    ls = functools.reduce(lambda a, b: a + b, w)
                    if not first:
                        ls = ls + l_s[n] * al
                    lss.append(ls)
                    if not last:
                        m_s[n] = m
                        l_s[n] = ls
                    ps.append(jnp.concatenate([t.astype(jnp.bfloat16) for t in w], axis=1))
                pv_all = lax.dot_general(jnp.concatenate(ps, axis=0), v, nn, preferred_element_type=jnp.float32)
                for g in range(G):
                    n = h * 8 + g0 + g
                    pv = pv_all[g * 128:(g + 1) * 128]
                    if not first:
                        pv = pv + acc_s[n] * als[g]
                    if not last:
                        acc_s[n] = pv
                    else:
                        tot = jnp.sum(lss[g], axis=1, keepdims=True)
                        o_s[:, cols(g)] = (pv / tot).astype(jnp.bfloat16)

        lax.fori_loop(0, KVH // per, step, 0)

    def both(slots, halves_):
        loads = [resp_cols(slots)] if slots else []
        loads += [prefix_cols(halves_)] if halves_ else []
        def load(off):
            return jnp.concatenate([f(off) for f in loads], axis=0) if len(loads) > 1 else loads[0](off)
        prefix_bias(list(enumerate(halves_)))

        def bias():
            rows = [rb_s[where_is[s]] for s in slots]
            if halves_:
                rows.append(jnp.broadcast_to(bias_s[0:1, :len(halves_) * 128], (128, len(halves_) * 128)))
            return jnp.concatenate(rows, axis=1) if len(rows) > 1 else rows[0]

        return load, bias, len(slots) + len(halves_)

    ready = {0: (), 1: n1, 2: n2, 3: n3, 4: m1, 5: m2, 6: m3, 7: xx}

    first_chip = x == 0
    where_is = {s: s for s in range(8)}
    where_is[10] = jnp.where(first_chip, 6, 4)
    where_is[11] = jnp.where(first_chip, 4, 6)

    def need(slots, halves_):
        for s in slots:
            if s == 10:
                got_if(first_chip, m3[1])
                got_if(x > 0, m1[1])
                continue
            if s == 11:
                got_if(first_chip, m1[1])
                got_if(x > 0, m3[1])
                relay_until(41)
                continue
            if s == 1:
                late_n1(0)
                late_n1(1)
            if s == 4:
                relay_until(41)
            if s == 2:
                relay_until(43)
            got(*ready[s])
        for d, part in halves_:
            if d == 0:
                got(*((pxa,), (pxb, pxc, pxd))[part])
            elif d == -1:
                got(*((pya[0], pya[1]), (pya[2], pya[3]))[part])
            elif d == 1:
                got(*((pyb[0], pyb[1]), (pyb[2], pyb[3]))[part])
            else:
                got(*((pyc[0], pyd[1]), (pyc[1], pyd[0], pyd[2]))[part])

    def chunk(t0, dt, slots, halves_, first=False, last=False, per=2):
        relay_until(t0)
        need(slots, halves_)
        load, bias_of, width = both(slots, [(y + d, part) for d, part in halves_])
        attend(load, bias_of, width, first, last, t0, dt, per)

    resp_bias(0)
    chunk(10, 0.5, (0,), (), first=True)
    chunk(17.8, 0.5, (), ((0, 0),))
    relay_until(25)
    all_resp_bias()
    chunk(27.5, 0.6, (7,), ((0, 1),))
    chunk(32.5, 0.6, (3,), ((1, 0),))
    chunk(37.5, 0.75, (1,), ((1, 1), (-1, 0)))
    relay_until(43)
    chunk(43.7, 0.6, (10, 2), (), per=4)
    relay_until(100)
    chunk(48.2, 0.6, (11,), ((-1, 1),), per=4)
    chunk(52, 0.75, (5,), ((2, 0), (2, 1)), last=True, per=4)
    for c, when in started:
        if when is None:
            c.wait_send()
        else:
            pl.when(when)(c.wait_send)


def on_device(queries, resp_kv, resp_segments, prefix_kv, tile_plan, prompt_lengths):
    anywhere = pl.BlockSpec(memory_space=pl.ANY)
    inside = pl.BlockSpec(memory_space=VMEM)
    out = pl.pallas_call(
        main_kernel,
        out_shape=jax.ShapeDtypeStruct((ROWS, H * HD), jnp.bfloat16),
        in_specs=[pl.BlockSpec(memory_space=pltpu.SMEM)] * 2 + [anywhere] * 4,
        out_specs=inside,
        scratch_shapes=[
            VMEM((ROWS, H * HD), jnp.bfloat16),
            VMEM((4, TILE, WIDE), jnp.bfloat16),
            VMEM((4, TILE, PWIDE), jnp.bfloat16),
            VMEM((9, ROWS, WIDE), jnp.bfloat16),
            VMEM((8, 1, 128), jnp.int32),
            VMEM((32, 32, PWIDE), jnp.bfloat16),
            VMEM((H, ROWS, 128), jnp.float32),
            VMEM((H, ROWS, 128), jnp.float32),
            VMEM((H, ROWS, 128), jnp.float32),
            VMEM((8, 512), jnp.float32),
            VMEM((8, ROWS, 128), jnp.float32),
            pltpu.SemaphoreType.DMA((NCOPY,)),
            pltpu.SemaphoreType.DMA((NCOPY,)),
            pltpu.SemaphoreType.DMA((5,)),
        ],
        compiler_params=pltpu.CompilerParams(
            collective_id=0, has_side_effects=True, vmem_limit_bytes=40 << 20
        ),
        name="attend",
    )(prompt_lengths, tile_plan.T, *(pltpu.with_memory_space_constraint(t, pltpu.HBM) for t in (queries[0], resp_kv[0], resp_segments, prefix_kv)))
    return out[None]


def solution(mesh):
    return jax.shard_map(
        on_device,
        mesh=mesh,
        in_specs=(
            P("prompt", "resp", None),
            P("prompt", "resp", None),
            P("prompt", "resp"),
            P(("prompt", "resp"), None, None),
            P(("prompt", "resp"), None),
            P("prompt"),
        ),
        out_specs=P("prompt", "resp", None),
        check_vma=False,
    )
```

```python
import functools
import math

import jax
import jax.numpy as jnp
from jax import lax
from jax.experimental import pallas as pl
from jax.experimental.pallas import tpu as pltpu
from jax.sharding import PartitionSpec as P

H = 64
KVH = 8
HD = 128
ROWS = 128
TILE = 8
WIDE = 2 * KVH * HD
NEG = -1e30
C = math.log2(math.e) / math.sqrt(HD)
MESH = pl.DeviceIdType.MESH
VMEM = pltpu.VMEM
G = 8


NCOPY = 80


def main_kernel(
    len_ref, plan_ref, q_hbm, kv_hbm, seg_hbm, prefix_hbm, o_s,
    q_s, raw, tiles, mark, mbuf, rbuf, sbuf, pbuf, m_s, l_s, acc_s, bias_s, rb_s,
    send, recv, local,
):
    p = lax.axis_index("prompt")
    r = lax.axis_index("resp")
    z = lax.rem(r, 2)
    x = lax.rem(r // 2, 4)
    y = r // 8

    def at(yy, xx, zz):
        return lax.rem(yy + 4, 4) * 8 + lax.rem(xx + 4, 4) * 2 + zz

    partner = r + 1 - 2 * z
    xp, xm, yp, ym = at(y, x + 1, z), at(y, x - 1, z), at(y + 1, x, z), at(y - 1, x, z)

    l_raw = pltpu.make_async_copy(prefix_hbm, raw, local.at[4])
    l_raw.start()
    barrier = pltpu.get_barrier_semaphore()
    for k in range(1, 4):
        q = lax.rem(p + k, 4)
        pl.semaphore_signal(barrier, inc=1, device_id={"prompt": q}, device_id_type=MESH)
        pl.semaphore_signal(barrier, inc=1, device_id={"prompt": q, "resp": partner}, device_id_type=MESH)
    for d in (partner, xp, xm, yp, ym):
        pl.semaphore_signal(barrier, inc=1, device_id={"resp": d}, device_id_type=MESH)

    l_q = pltpu.make_async_copy(q_hbm, q_s, local.at[0])
    l_kv = pltpu.make_async_copy(kv_hbm, rbuf.at[0], local.at[1])
    l_seg = pltpu.make_async_copy(seg_hbm, sbuf.at[0], local.at[2])
    l_tile = pltpu.make_async_copy(tiles.at[p], pbuf.at[r, pl.ds(pl.multiple_of(p * 8, 8), 8)], local.at[3])
    l_kv.start()
    l_seg.start()
    l_q.start()
    l_raw.wait()
    for q in range(4):
        slot = jnp.int32(0)
        place = jnp.int32(0)
        for t in range(4):
            hit = plan_ref[0, t] == q
            slot = jnp.where(hit, t, slot)
            place = jnp.where(hit, plan_ref[1, t], place)
        tiles[q] = raw[slot]
        mark[q] = jnp.full((1, 128), place, jnp.int32)
    l_kv.wait()
    l_seg.wait()
    pl.semaphore_wait(barrier, 11)
    l_mark = pltpu.make_async_copy(mark.at[p], mbuf.at[r, p], local.at[5])
    l_tile.start()
    l_mark.start()

    counter = [0]
    started = []

    def copy(src, dst, to, when=None, recv_as=None):
        i = counter[0]
        counter[0] += 1
        assert i < NCOPY
        c = pltpu.make_async_remote_copy(
            src_ref=src, dst_ref=dst, send_sem=send.at[i], recv_sem=recv.at[i if recv_as is None else recv_as],
            device_id=to, device_id_type=MESH,
        )
        started.append((c, when))
        c_index[id(c)] = i
        return c

    c_index = {}

    def rs(d):
        return {"resp": d}

    def flat(cs):
        return [d for c in cs for d in (flat(c) if isinstance(c, (list, tuple)) else (c,))]

    def start(*cs, when=None):
        def go():
            for c in flat(cs):
                c.start()
        if when is None:
            go()
        else:
            pl.when(when)(go)

    waited = set()

    def got(*cs):
        for c in flat(cs):
            if id(c) not in waited:
                waited.add(id(c))
                c.wait_recv()

    halves = (pl.ds(0, 64), pl.ds(64, 64))
    OWN, ROWB = 0, 8
    def tile_at():
        return pbuf.at[r, pl.ds(pl.multiple_of(p * 8, 8), 8)]

    p0 = []
    for k in range(1, 4):
        q = lax.rem(p + k, 4)
        p0.append(copy(tiles.at[q], tile_at(), {"prompt": q}))
        p0.append(copy(tiles.at[q], tile_at(), {"prompt": q, "resp": partner}))
        p0.append(copy(mark.at[q], mbuf.at[r, p], {"prompt": q}))
        p0.append(copy(mark.at[q], mbuf.at[r, p], {"prompt": q, "resp": partner}))
    p0.append(copy(tiles.at[p], tile_at(), rs(partner)))
    p0.append(copy(mark.at[p], mbuf.at[r, p], rs(partner)))

    def block(src, dst, h, to, when=None, recv_as=None):
        first = recv_as if recv_as is None else recv_as[0]
        out = [copy(rbuf.at[src, halves[h]], rbuf.at[dst, halves[h]], to, when, first and c_index[id(first)])]
        if h == 0:
            second = recv_as if recv_as is None else recv_as[1]
            out.append(copy(sbuf.at[src], sbuf.at[dst], to, when, second and c_index[id(second)]))
        return out

    src1 = jnp.where(x == 3, ROWB, OWN)
    src3 = jnp.where(x == 0, OWN, ROWB)
    src7 = jnp.where(z == 0, OWN, ROWB)
    both_halves = (0, 1)
    tt = [block(OWN, ROWB, h, rs(yp)) for h in both_halves]
    n1 = [block(src1, 1, h, rs(xp)) for h in both_halves]
    n3 = [block(src3, 3, h, rs(xm)) for h in both_halves]
    xx = [block(src7, 7, h, rs(partner)) for h in both_halves]
    m1 = [block(1, 4, h, rs(partner)) for h in both_halves]
    m3 = [block(3, 6, h, rs(partner)) for h in both_halves]
    n2 = [block(1, 2, 0, rs(xp), x < 3), block(3, 2, 1, rs(xm), x > 0)]
    n2x = [block(3, 2, 0, rs(xm), x == 1, n2[0]), block(1, 2, 1, rs(xp), x == 2, n2[1])]
    m2 = [block(4, 5, 0, rs(xp), x < 3), block(2, 5, 1, rs(partner))]
    m2x = block(6, 5, 0, rs(xm), x == 1, m2[0])

    def pair(yy, xx_, to):
        span = pl.ds(at(yy, xx_, 0), 2)
        return [copy(t.at[span], t.at[span], to) for t in (pbuf, mbuf)]

    def one(yy, xx_, zz, to):
        i = at(yy, xx_, zz)
        return [copy(t.at[i], t.at[i], to) for t in (pbuf, mbuf)]

    pxa = pair(y, x, rs(xp))
    pxb = pair(y, x, rs(xm))
    pxc = one(y, x - 1, 0, rs(xp))
    pxd = one(y, x + 1, 1, rs(xm))
    offs = (0, -1, 1, 2)
    pya = [pair(y, x + o, rs(yp)) for o in offs]
    pyb = [pair(y, x + o, rs(ym)) for o in offs]
    pyc = [pair(y - 1, x, rs(yp)), one(y - 1, x + 1, 0, rs(yp))]
    pyd = [one(y + 1, x + 1, 1, rs(ym)), pair(y + 1, x - 1, rs(ym)), pair(y + 1, x + 2, rs(ym))]

    start(*p0, *tt)
    start(n1[0], when=x < 3)
    start(n3[0], when=x == 0)
    start(*xx, when=z == 0)
    l_tile.wait()
    l_mark.wait()
    got(*p0)
    start(pxa, pxb, pyb[0], pya[0])
    start(n1[1], when=x < 3)
    start(n3[1], when=x == 0)
    l_q.wait()

    def got_if(cond, c):
        for d in flat([c]):
            waited.add(id(d))
            pl.when(cond)(d.wait_recv)

    def relay_t(i):
        got(tt[i])
        start(n1[i], when=x == 3)
        start(n3[i], when=x > 0)
        start(xx[i], when=z == 1)

    def relay_pa():
        got(pxa)
        start(pxc, pyb[1], pya[1])

    def relay_pb():
        got(pxb)
        start(pxd, pyb[2], pya[2])

    def relay_pc():
        got(pxc, pxd)
        start(pyb[3], pya[3])

    def take_n1(i, cond):
        got_if(cond, n1[i])
        start(m1[i], when=cond)

    late = set()

    def late_n1(i):
        if i not in late:
            late.add(i)
            take_n1(i, x == 0)
            if i == 0:
                start(n2[0], when=x == 0)

    def send_n2(i):
        if i == 0:
            start(n2[0], when=x < 3)
        else:
            start(n2x[1], when=x == 2)

    def relay_n3(i):
        got(n3[i])
        if i == 0:
            start(n2x[0], when=x == 1)
        else:
            start(n2[1], when=x > 0)
        start(m3[i])

    def relay_m1(cond):
        got_if(cond, m1[0])
        start(m2[0], when=cond & (x < 3))

    def relay_m3():
        got(m3[0])
        start(m2x, when=x == 1)

    def relay_n2(cond):
        got_if(cond, n2[1])
        start(m2[1], when=cond)

    def relay_ya(i):
        got(pya[i])
        if i == 0:
            start(pyc[0])
        if i == 2:
            start(pyc[1])

    def relay_yb(i):
        got(pyb[i])
        if i == 2:
            start(pyd[0])
        if i == 1:
            start(pyd[1])
        if i == 3:
            start(pyd[2])

    relays = [
        (11.5, lambda: relay_t(0)),
        (12, lambda: take_n1(0, x > 0)),
        (17, lambda: relay_pb()),
        (17.2, lambda: relay_pa()),
        (17.5, lambda: relay_t(1)),
        (17.6, lambda: pl.when(x > 0)(lambda: send_n2(0))),
        (22, lambda: relay_n3(0)),
        (22.6, lambda: late_n1(0)),
        (23, lambda: relay_ya(0)),
        (24, lambda: take_n1(1, x > 0)),
        (25.8, lambda: relay_pc()),
        (25.9, lambda: send_n2(1)),
        (26, lambda: relay_yb(2)),
        (29, lambda: relay_ya(2)),
                (31.2, lambda: relay_n3(1)),
        (31.4, lambda: relay_m1(x > 0)),
        (32, lambda: relay_yb(1)),
        (33.5, lambda: late_n1(1)),
        (37.5, lambda: relay_yb(3)),
        (38, lambda: relay_n2(x > 0)),
        (38.5, lambda: relay_m3()),
        (41, lambda: relay_m1(x == 0)),
        (43, lambda: relay_n2(x == 0)),
    ]

    def due(t):
        fns = []
        while relays and relays[0][0] <= t:
            fns.append(relays.pop(0)[1])
        return fns

    def relay_until(t):
        for f in due(t):
            f()

    seg_own = jnp.transpose(jnp.broadcast_to(sbuf[0].astype(jnp.float32), (128, 128)))
    row = lax.broadcasted_iota(jnp.int32, (128, 128), 0)
    col = lax.broadcasted_iota(jnp.int32, (128, 128), 1)

    def resp_bias(s):
        if s == 0:
            d = jnp.int32(0)
        elif s <= 3:
            d = jnp.int32(2 * s)
        elif s <= 6:
            d = 2 * (s - 3) - 1 + 2 * z
        else:
            d = 7 - 6 * z
        theirs = sbuf[s].astype(jnp.float32)
        theirs = jnp.where(r >= d, theirs, -1.0)
        ok = seg_own == theirs
        if s == 0:
            ok = ok & (col <= row)
        rb_s[s] = jnp.where(ok, 0.0, NEG)

    masked = set()

    def resp_biases(slots):
        for s in [t for u in slots for t in ((4, 6) if u in (10, 11) else (u,))]:
            if s not in masked:
                masked.add(s)
                resp_bias(s)

    def tiles_of(pairs, lanes):
        return jnp.concatenate([pbuf[pl.ds(at(y + d, x + o, 0), 2), :, lanes].reshape(64, 128) for d, o in pairs], axis=0)

    def prefix_bias(groups):
        limit = len_ref[0]
        lane = lax.broadcasted_iota(jnp.int32, (1, 128), 1)
        for j, pairs in groups:
            places = jnp.zeros((1, 128), jnp.int32)
            for i, (d, o) in enumerate(pairs):
                for k in range(8):
                    m = mbuf[at(y + d, x + o, k // 4), k % 4]
                    places = jnp.where(lane // 8 == i * 8 + k, m, places)
            pos = places * 8 + lax.rem(lane, 8)
            bias_s[:, j * 128:(j + 1) * 128] = jnp.broadcast_to(jnp.where(pos < limit, 0.0, NEG), (8, 128))

    def resp_cols(slots):
        def load(off):
            return jnp.concatenate([rbuf[where_is[s], :, pl.ds(off, 128)] for s in slots], axis=0)
        return load

    def prefix_cols(halves_):
        def load(off):
            return jnp.concatenate([tiles_of(pairs, pl.ds(off, 128)) for pairs in halves_], axis=0)
        return load

    nt = (((1,), (1,)), ((), ()))
    nn = (((1,), (0,)), ((), ()))

    def attend(load, bias_of, width, first, last, t0, dt, per):
        hooks = [(i, due(t0 + per * i * dt)) for i in range(KVH // per)]
        hooks = [(i, fns) for i, fns in hooks if fns]

        def step(i, carry):
            for j, fns in hooks:
                def run(fns=fns):
                    for f in fns:
                        f()
                pl.when(i == j)(run)
            for j in range(per):
                head(per * i + j)
            return carry

        def head(h):
            off = pl.multiple_of(h * 128, 128)
            k = load(off)
            v = load(pl.multiple_of(off + KVH * HD, 128))
            bias = bias_of()
            for g0 in range(0, 8, G):
                def cols(g):
                    return pl.ds(pl.multiple_of(off * 8 + (g0 + g) * 128, 128), 128)
                qs = jnp.concatenate([q_s[:, cols(g)] for g in range(G)], axis=0)
                scores = lax.dot_general(qs, k, nt, preferred_element_type=jnp.float32)
                ps, als, lss = [], [], []
                for g in range(G):
                    n = h * 8 + g0 + g
                    s = scores[g * 128:(g + 1) * 128] + bias
                    parts = [s[:, j * 128:(j + 1) * 128] for j in range(width)]
                    mx = jnp.max(functools.reduce(jnp.maximum, parts), axis=1, keepdims=True)
                    if first:
                        m = jnp.broadcast_to(mx, (128, 128))
                    else:
                        mo = m_s[n]
                        m = jnp.maximum(mo, mx)
                        al = jnp.exp2((mo - m) * C)
                        als.append(al)
                    w = [jnp.exp2((t - m) * C) for t in parts]
                    ls = functools.reduce(lambda a, b: a + b, w)
                    if not first:
                        ls = ls + l_s[n] * al
                    lss.append(ls)
                    if not last:
                        m_s[n] = m
                        l_s[n] = ls
                    ps.append(jnp.concatenate([t.astype(jnp.bfloat16) for t in w], axis=1))
                pv_all = lax.dot_general(jnp.concatenate(ps, axis=0), v, nn, preferred_element_type=jnp.float32)
                for g in range(G):
                    n = h * 8 + g0 + g
                    pv = pv_all[g * 128:(g + 1) * 128]
                    if not first:
                        pv = pv + acc_s[n] * als[g]
                    if not last:
                        acc_s[n] = pv
                    else:
                        tot = jnp.sum(lss[g], axis=1, keepdims=True)
                        o_s[:, cols(g)] = (pv / tot).astype(jnp.bfloat16)

        lax.fori_loop(0, KVH // per, step, 0)

    def both(slots, halves_):
        loads = [resp_cols(slots)] if slots else []
        loads += [prefix_cols(halves_)] if halves_ else []
        def load(off):
            return jnp.concatenate([f(off) for f in loads], axis=0) if len(loads) > 1 else loads[0](off)
        resp_biases(slots)
        prefix_bias(list(enumerate(halves_)))

        def bias():
            rows = [rb_s[where_is[s]] for s in slots]
            if halves_:
                rows.append(jnp.broadcast_to(bias_s[0:1, :len(halves_) * 128], (128, len(halves_) * 128)))
            return jnp.concatenate(rows, axis=1) if len(rows) > 1 else rows[0]

        return load, bias, len(slots) + len(halves_)

    ready = {0: (), 1: n1, 2: n2, 3: n3, 4: m1, 5: m2, 6: m3, 7: xx}

    pieces = {(0, 0): (), (0, -1): pxa, (0, 1): pxb, (0, 2): (pxc, pxd)}
    for i, o in enumerate(offs):
        pieces[-1, o], pieces[1, o] = pya[i], pyb[i]
    pieces[2, 0], pieces[2, -1], pieces[2, 1], pieces[2, 2] = pyc[0], pyd[1], (pyc[1], pyd[0]), pyd[2]
    first_chip = x == 0
    where_is = {s: s for s in range(8)}
    where_is[10] = jnp.where(first_chip, 6, 4)
    where_is[11] = jnp.where(first_chip, 4, 6)

    def need(slots, halves_):
        for s in slots:
            if s == 10:
                got(m3[0])
                got_if(first_chip, m3[1])
                got_if(x > 0, m1[1])
                continue
            if s == 11:
                got_if(first_chip, m1[1])
                got_if(x > 0, m3[1])
                relay_until(41)
                continue
            if s == 1:
                late_n1(0)
                late_n1(1)
            if s == 4:
                relay_until(41)
            if s == 2:
                relay_until(43)
            got(*ready[s])
        for pairs in halves_:
            for d, o in pairs:
                got(pieces[d, o])

    def chunk(t0, dt, slots, halves_, first=False, last=False, per=2):
        relay_until(t0)
        need(slots, halves_)
        load, bias_of, width = both(slots, halves_)
        attend(load, bias_of, width, first, last, t0, dt, per)

    chunk(10, 0.5, (0,), (), first=True)
    chunk(17.2, 0.5, (), (((0, 0), (0, -1)),))
    relay_until(23.4)
    chunk(23.5, 0.5, (), (((1, 0), (-1, 0)),))
    chunk(27.5, 0.6, (7,), (((0, 1), (0, 2)),))
    chunk(32, 0.6, (3,), (((1, 1), (-1, 1)),))
    chunk(36.5, 0.6, (1,), (((1, -1), (-1, -1)),))
    relay_until(43)
    chunk(42, 0.6, (10, 2), (), per=4)
    relay_until(100)
    chunk(46.5, 0.6, (11,), (((1, 2), (-1, 2)),), per=4)
    chunk(51, 0.75, (5,), (((2, 0), (2, -1)), ((2, 1), (2, 2))), last=True, per=4)
    for c, when in started:
        if when is None:
            c.wait_send()
        else:
            pl.when(when)(c.wait_send)


def on_device(queries, resp_kv, resp_segments, prefix_kv, tile_plan, prompt_lengths):
    anywhere = pl.BlockSpec(memory_space=pl.ANY)
    inside = pl.BlockSpec(memory_space=VMEM)
    out = pl.pallas_call(
        main_kernel,
        out_shape=jax.ShapeDtypeStruct((ROWS, H * HD), jnp.bfloat16),
        in_specs=[pl.BlockSpec(memory_space=pltpu.SMEM)] * 2 + [anywhere] * 4,
        out_specs=inside,
        scratch_shapes=[
            VMEM((ROWS, H * HD), jnp.bfloat16),
            VMEM((4, TILE, WIDE), jnp.bfloat16),
            VMEM((4, TILE, WIDE), jnp.bfloat16),
            VMEM((4, 1, 128), jnp.int32),
            VMEM((32, 4, 1, 128), jnp.int32),
            VMEM((9, ROWS, WIDE), jnp.bfloat16),
            VMEM((9, 1, 128), jnp.int32),
            VMEM((32, 32, WIDE), jnp.bfloat16),
            VMEM((H, ROWS, 128), jnp.float32),
            VMEM((H, ROWS, 128), jnp.float32),
            VMEM((H, ROWS, 128), jnp.float32),
            VMEM((8, 512), jnp.float32),
            VMEM((8, ROWS, 128), jnp.float32),
            pltpu.SemaphoreType.DMA((NCOPY,)),
            pltpu.SemaphoreType.DMA((NCOPY,)),
            pltpu.SemaphoreType.DMA((6,)),
        ],
        compiler_params=pltpu.CompilerParams(
            collective_id=0, has_side_effects=True, vmem_limit_bytes=40 << 20
        ),
        name="attend",
    )(prompt_lengths, tile_plan.T, *(pltpu.with_memory_space_constraint(t, pltpu.HBM) for t in (queries[0], resp_kv[0], resp_segments, prefix_kv)))
    return out[None]


def solution(mesh):
    return jax.shard_map(
        on_device,
        mesh=mesh,
        in_specs=(
            P("prompt", "resp", None),
            P("prompt", "resp", None),
            P("prompt", "resp"),
            P(("prompt", "resp"), None, None),
            P(("prompt", "resp"), None),
            P("prompt"),
        ),
        out_specs=P("prompt", "resp", None),
        check_vma=False,
    )
```

```python
import functools
import math

import jax
import jax.numpy as jnp
from jax import lax
from jax.experimental import pallas as pl
from jax.experimental.pallas import tpu as pltpu
from jax.sharding import PartitionSpec as P

H = 64
KVH = 8
HD = 128
ROWS = 128
TILE = 8
WIDE = 2 * KVH * HD
NEG = -1e30
C = math.log2(math.e) / math.sqrt(HD)
MESH = pl.DeviceIdType.MESH
VMEM = pltpu.VMEM
G = 8


NCOPY = 80


def main_kernel(
    len_ref, plan_ref, q_hbm, kv_hbm, seg_hbm, prefix_hbm, o_s,
    q_s, raw, tiles, mark, mbuf, rbuf, sbuf, pbuf, m_s, l_s, acc_s, bias_s, rb_s,
    send, recv, local,
):
    p = lax.axis_index("prompt")
    r = lax.axis_index("resp")
    z = lax.rem(r, 2)
    x = lax.rem(r // 2, 4)
    y = r // 8

    def at(yy, xx, zz):
        return lax.rem(yy + 4, 4) * 8 + lax.rem(xx + 4, 4) * 2 + zz

    partner = r + 1 - 2 * z
    xp, xm, yp, ym = at(y, x + 1, z), at(y, x - 1, z), at(y + 1, x, z), at(y - 1, x, z)

    l_raw = pltpu.make_async_copy(prefix_hbm, raw, local.at[4])
    l_raw.start()
    barrier = pltpu.get_barrier_semaphore()
    for k in range(1, 4):
        q = lax.rem(p + k, 4)
        pl.semaphore_signal(barrier, inc=1, device_id={"prompt": q}, device_id_type=MESH)
        pl.semaphore_signal(barrier, inc=1, device_id={"prompt": q, "resp": partner}, device_id_type=MESH)
    for d in (partner, xp, xm, yp, ym):
        pl.semaphore_signal(barrier, inc=1, device_id={"resp": d}, device_id_type=MESH)

    l_q = pltpu.make_async_copy(q_hbm, q_s, local.at[0])
    l_kv = pltpu.make_async_copy(kv_hbm, rbuf.at[0], local.at[1])
    l_seg = pltpu.make_async_copy(seg_hbm, sbuf.at[0], local.at[2])
    l_tile = pltpu.make_async_copy(tiles.at[p], pbuf.at[r, pl.ds(pl.multiple_of(p * 8, 8), 8)], local.at[3])
    l_kv.start()
    l_seg.start()
    l_q.start()
    l_raw.wait()
    for q in range(4):
        slot = jnp.int32(0)
        place = jnp.int32(0)
        for t in range(4):
            hit = plan_ref[0, t] == q
            slot = jnp.where(hit, t, slot)
            place = jnp.where(hit, plan_ref[1, t], place)
        tiles[q] = raw[slot]
        mark[q] = jnp.full((1, 128), place, jnp.int32)
    l_kv.wait()
    l_seg.wait()
    pl.semaphore_wait(barrier, 11)
    l_mark = pltpu.make_async_copy(mark.at[p], mbuf.at[r, p], local.at[5])
    l_tile.start()
    l_mark.start()

    counter = [0]
    started = []

    def copy(src, dst, to, when=None, recv_as=None):
        i = counter[0]
        counter[0] += 1
        assert i < NCOPY
        c = pltpu.make_async_remote_copy(
            src_ref=src, dst_ref=dst, send_sem=send.at[i], recv_sem=recv.at[i if recv_as is None else recv_as],
            device_id=to, device_id_type=MESH,
        )
        started.append((c, when))
        c_index[id(c)] = i
        return c

    c_index = {}

    def rs(d):
        return {"resp": d}

    def flat(cs):
        return [d for c in cs for d in (flat(c) if isinstance(c, (list, tuple)) else (c,))]

    def start(*cs, when=None):
        def go():
            for c in flat(cs):
                c.start()
        if when is None:
            go()
        else:
            pl.when(when)(go)

    waited = set()

    def got(*cs):
        for c in flat(cs):
            if id(c) not in waited:
                waited.add(id(c))
                c.wait_recv()

    halves = (pl.ds(0, 64), pl.ds(64, 64))
    OWN, ROWB = 0, 8
    def tile_at():
        return pbuf.at[r, pl.ds(pl.multiple_of(p * 8, 8), 8)]

    p0 = []
    for k in range(1, 4):
        q = lax.rem(p + k, 4)
        p0.append(copy(tiles.at[q], tile_at(), {"prompt": q}))
        p0.append(copy(tiles.at[q], tile_at(), {"prompt": q, "resp": partner}))
        p0.append(copy(mark.at[q], mbuf.at[r, p], {"prompt": q}))
        p0.append(copy(mark.at[q], mbuf.at[r, p], {"prompt": q, "resp": partner}))
    p0.append(copy(tiles.at[p], tile_at(), rs(partner)))
    p0.append(copy(mark.at[p], mbuf.at[r, p], rs(partner)))

    def block(src, dst, h, to, when=None, recv_as=None):
        first = recv_as if recv_as is None else recv_as[0]
        out = [copy(rbuf.at[src, halves[h]], rbuf.at[dst, halves[h]], to, when, first and c_index[id(first)])]
        if h == 0:
            second = recv_as if recv_as is None else recv_as[1]
            out.append(copy(sbuf.at[src], sbuf.at[dst], to, when, second and c_index[id(second)]))
        return out

    src1 = jnp.where(x == 3, ROWB, OWN)
    src3 = jnp.where(x == 0, OWN, ROWB)
    src7 = jnp.where(z == 0, OWN, ROWB)
    both_halves = (0, 1)
    tt = [block(OWN, ROWB, h, rs(yp)) for h in both_halves]
    n1 = [block(src1, 1, h, rs(xp)) for h in both_halves]
    n3 = [block(src3, 3, h, rs(xm)) for h in both_halves]
    xx = [block(src7, 7, h, rs(partner)) for h in both_halves]
    m1 = [block(1, 4, h, rs(partner)) for h in both_halves]
    m3 = [block(3, 6, h, rs(partner)) for h in both_halves]
    n2 = [block(1, 2, 0, rs(xp), x < 3), block(3, 2, 1, rs(xm), x > 0)]
    n2x = [block(3, 2, 0, rs(xm), x == 1, n2[0]), block(1, 2, 1, rs(xp), x == 2, n2[1])]
    m2 = [block(4, 5, 0, rs(xp), x < 3), block(2, 5, 1, rs(partner))]
    m2x = block(6, 5, 0, rs(xm), x == 1, m2[0])

    def pair(yy, xx_, to):
        span = pl.ds(at(yy, xx_, 0), 2)
        return [copy(t.at[span], t.at[span], to) for t in (pbuf, mbuf)]

    def one(yy, xx_, zz, to):
        i = at(yy, xx_, zz)
        return [copy(t.at[i], t.at[i], to) for t in (pbuf, mbuf)]

    pxa = pair(y, x, rs(xp))
    pxb = pair(y, x, rs(xm))
    pxc = one(y, x - 1, 0, rs(xp))
    pxd = one(y, x + 1, 1, rs(xm))
    offs = (0, -1, 1, 2)
    pya = [pair(y, x + o, rs(yp)) for o in offs]
    pyb = [pair(y, x + o, rs(ym)) for o in offs]
    pyc = [pair(y - 1, x, rs(yp)), one(y - 1, x + 1, 0, rs(yp))]
    pyd = [one(y + 1, x + 1, 1, rs(ym)), pair(y + 1, x - 1, rs(ym)), pair(y + 1, x + 2, rs(ym))]

    start(*p0, *tt)
    start(n1[0], when=x < 3)
    start(n3[0], when=x == 0)
    start(*xx, when=z == 0)
    l_tile.wait()
    l_mark.wait()
    got(*p0)
    start(pxa, pxb, pyb[0], pya[0])
    start(n1[1], when=x < 3)
    start(n3[1], when=x == 0)
    l_q.wait()

    def got_if(cond, c):
        for d in flat([c]):
            waited.add(id(d))
            pl.when(cond)(d.wait_recv)

    def relay_t(i):
        got(tt[i])
        start(n1[i], when=x == 3)
        start(n3[i], when=x > 0)
        start(xx[i], when=z == 1)

    def relay_pa():
        got(pxa)
        start(pxc, pyb[1], pya[1])

    def relay_pb():
        got(pxb)
        start(pxd, pyb[2], pya[2])

    def relay_pc():
        got(pxc, pxd)
        start(pyb[3], pya[3])

    def take_n1(i, cond):
        got_if(cond, n1[i])
        start(m1[i], when=cond)

    late = set()

    def late_n1(i):
        if i not in late:
            late.add(i)
            take_n1(i, x == 0)
            if i == 0:
                start(n2[0], when=x == 0)

    def send_n2(i):
        if i == 0:
            start(n2[0], when=x < 3)
        else:
            start(n2x[1], when=x == 2)

    def relay_n3(i):
        got(n3[i])
        if i == 0:
            start(n2x[0], when=x == 1)
        else:
            start(n2[1], when=x > 0)
        start(m3[i])

    def relay_m1(cond):
        got_if(cond, m1[0])
        start(m2[0], when=cond & (x < 3))

    def relay_m3():
        got(m3[0])
        start(m2x, when=x == 1)

    def relay_n2(cond):
        got_if(cond, n2[1])
        start(m2[1], when=cond)

    def relay_ya(i):
        got(pya[i])
        if i == 0:
            start(pyc[0])
        if i == 2:
            start(pyc[1])

    def relay_yb(i):
        got(pyb[i])
        if i == 2:
            start(pyd[0])
        if i == 1:
            start(pyd[1])
        if i == 3:
            start(pyd[2])

    relays = [
        (11.5, lambda: relay_t(0)),
        (12, lambda: take_n1(0, x > 0)),
        (17, lambda: relay_pb()),
        (17.2, lambda: relay_pa()),
        (17.5, lambda: relay_t(1)),
        (17.6, lambda: pl.when(x > 0)(lambda: send_n2(0))),
        (22, lambda: relay_n3(0)),
        (22.6, lambda: late_n1(0)),
        (23, lambda: relay_ya(0)),
        (24, lambda: take_n1(1, x > 0)),
        (25.8, lambda: relay_pc()),
        (25.9, lambda: send_n2(1)),
        (26, lambda: relay_yb(2)),
        (29, lambda: relay_ya(2)),
                (31.2, lambda: relay_n3(1)),
        (31.4, lambda: relay_m1(x > 0)),
        (32, lambda: relay_yb(1)),
        (33.5, lambda: late_n1(1)),
        (37.5, lambda: relay_yb(3)),
        (38, lambda: relay_n2(x > 0)),
        (38.5, lambda: relay_m3()),
        (41, lambda: relay_m1(x == 0)),
        (43, lambda: relay_n2(x == 0)),
    ]

    def due(t):
        fns = []
        while relays and relays[0][0] <= t:
            fns.append(relays.pop(0)[1])
        return fns

    def relay_until(t):
        for f in due(t):
            f()

    seg_own = jnp.transpose(jnp.broadcast_to(sbuf[0].astype(jnp.float32), (128, 128)))
    row = lax.broadcasted_iota(jnp.int32, (128, 128), 0)
    col = lax.broadcasted_iota(jnp.int32, (128, 128), 1)

    def resp_bias(s):
        if s == 0:
            d = jnp.int32(0)
        elif s <= 3:
            d = jnp.int32(2 * s)
        elif s <= 6:
            d = 2 * (s - 3) - 1 + 2 * z
        else:
            d = 7 - 6 * z
        theirs = sbuf[s].astype(jnp.float32)
        theirs = jnp.where(r >= d, theirs, -1.0)
        ok = seg_own == theirs
        if s == 0:
            ok = ok & (col <= row)
        rb_s[s] = jnp.where(ok, 0.0, NEG)

    masked = set()

    def resp_biases(slots):
        for s in [t for u in slots for t in ((4, 6) if u in (10, 11) else (u,))]:
            if s not in masked:
                masked.add(s)
                resp_bias(s)

    def tiles_of(pairs, lanes):
        return jnp.concatenate([pbuf[pl.ds(at(y + d, x + o, 0), 2), :, lanes].reshape(64, 128) for d, o in pairs], axis=0)

    def prefix_bias(groups):
        limit = len_ref[0]
        lane = lax.broadcasted_iota(jnp.int32, (1, 128), 1)
        for j, pairs in groups:
            places = jnp.zeros((1, 128), jnp.int32)
            for i, (d, o) in enumerate(pairs):
                for k in range(8):
                    m = mbuf[at(y + d, x + o, k // 4), k % 4]
                    places = jnp.where(lane // 8 == i * 8 + k, m, places)
            pos = places * 8 + lax.rem(lane, 8)
            bias_s[:, j * 128:(j + 1) * 128] = jnp.broadcast_to(jnp.where(pos < limit, 0.0, NEG), (8, 128))

    def resp_cols(slots):
        def load(off):
            return jnp.concatenate([rbuf[where_is[s], :, pl.ds(off, 128)] for s in slots], axis=0)
        return load

    def prefix_cols(halves_):
        def load(off):
            return jnp.concatenate([tiles_of(pairs, pl.ds(off, 128)) for pairs in halves_], axis=0)
        return load

    nt = (((1,), (1,)), ((), ()))
    nn = (((1,), (0,)), ((), ()))

    def attend(load, bias_of, width, first, last, t0, dt, per):
        hooks = [(i, due(t0 + per * i * dt)) for i in range(KVH // per)]
        hooks = [(i, fns) for i, fns in hooks if fns]

        def step(i, carry):
            for j, fns in hooks:
                def run(fns=fns):
                    for f in fns:
                        f()
                pl.when(i == j)(run)
            for j in range(per):
                head(per * i + j)
            return carry

        def head(h):
            off = pl.multiple_of(h * 128, 128)
            k = load(off)
            v = load(pl.multiple_of(off + KVH * HD, 128))
            bias = bias_of()
            for g0 in range(0, 8, G):
                def cols(g):
                    return pl.ds(pl.multiple_of(off * 8 + (g0 + g) * 128, 128), 128)
                qs = jnp.concatenate([q_s[:, cols(g)] for g in range(G)], axis=0)
                scores = lax.dot_general(qs, k, nt, preferred_element_type=jnp.float32)
                ps, als, lss = [], [], []
                for g in range(G):
                    n = h * 8 + g0 + g
                    s = scores[g * 128:(g + 1) * 128] + bias
                    parts = [s[:, j * 128:(j + 1) * 128] for j in range(width)]
                    mx = jnp.max(functools.reduce(jnp.maximum, parts), axis=1, keepdims=True)
                    if first:
                        m = jnp.broadcast_to(mx, (128, 128))
                    else:
                        mo = m_s[n]
                        m = jnp.maximum(mo, mx)
                        al = jnp.exp2((mo - m) * C)
                        als.append(al)
                    w = [jnp.exp2((t - m) * C) for t in parts]
                    ls = functools.reduce(lambda a, b: a + b, w)
                    if not first:
                        ls = ls + l_s[n] * al
                    lss.append(ls)
                    if not last:
                        m_s[n] = m
                        l_s[n] = ls
                    ps.append(jnp.concatenate([t.astype(jnp.bfloat16) for t in w], axis=1))
                pv_all = lax.dot_general(jnp.concatenate(ps, axis=0), v, nn, preferred_element_type=jnp.float32)
                for g in range(G):
                    n = h * 8 + g0 + g
                    pv = pv_all[g * 128:(g + 1) * 128]
                    if not first:
                        pv = pv + acc_s[n] * als[g]
                    if not last:
                        acc_s[n] = pv
                    else:
                        tot = jnp.sum(lss[g], axis=1, keepdims=True)
                        o_s[:, cols(g)] = (pv / tot).astype(jnp.bfloat16)

        lax.fori_loop(0, KVH // per, step, 0)

    def both(slots, halves_):
        loads = [resp_cols(slots)] if slots else []
        loads += [prefix_cols(halves_)] if halves_ else []
        def load(off):
            return jnp.concatenate([f(off) for f in loads], axis=0) if len(loads) > 1 else loads[0](off)
        resp_biases(slots)
        prefix_bias(list(enumerate(halves_)))

        def bias():
            rows = [rb_s[where_is[s]] for s in slots]
            if halves_:
                rows.append(jnp.broadcast_to(bias_s[0:1, :len(halves_) * 128], (128, len(halves_) * 128)))
            return jnp.concatenate(rows, axis=1) if len(rows) > 1 else rows[0]

        return load, bias, len(slots) + len(halves_)

    ready = {0: (), 1: n1, 2: n2, 3: n3, 4: m1, 5: m2, 6: m3, 7: xx}

    pieces = {(0, 0): (), (0, -1): pxa, (0, 1): pxb, (0, 2): (pxc, pxd)}
    for i, o in enumerate(offs):
        pieces[-1, o], pieces[1, o] = pya[i], pyb[i]
    pieces[2, 0], pieces[2, -1], pieces[2, 1], pieces[2, 2] = pyc[0], pyd[1], (pyc[1], pyd[0]), pyd[2]
    first_chip = x == 0
    where_is = {s: s for s in range(8)}
    where_is[10] = jnp.where(first_chip, 6, 4)
    where_is[11] = jnp.where(first_chip, 4, 6)

    def need(slots, halves_):
        for s in slots:
            if s == 10:
                got(m3[0])
                got_if(first_chip, m3[1])
                got_if(x > 0, m1[1])
                continue
            if s == 11:
                got_if(first_chip, m1[1])
                got_if(x > 0, m3[1])
                relay_until(41)
                continue
            if s == 1:
                late_n1(0)
                late_n1(1)
            if s == 4:
                relay_until(41)
            if s == 2:
                relay_until(43)
            got(*ready[s])
        for pairs in halves_:
            for d, o in pairs:
                got(pieces[d, o])

    def chunk(t0, dt, slots, halves_, first=False, last=False, per=2):
        relay_until(t0)
        need(slots, halves_)
        load, bias_of, width = both(slots, halves_)
        attend(load, bias_of, width, first, last, t0, dt, per)

    chunk(10, 0.5, (0,), (), first=True)
    chunk(17.2, 0.5, (), (((0, 0), (0, -1)),))
    relay_until(23.4)
    chunk(23.5, 0.5, (), (((1, 0), (-1, 0)),))
    chunk(27.5, 0.6, (7,), (((0, 1), (0, 2)),))
    chunk(32, 0.6, (3,), (((1, 1), (-1, 1)),))
    chunk(36.5, 0.6, (1,), (((1, -1), (-1, -1)),))
    relay_until(43)
    chunk(42, 0.6, (10, 2), (), per=4)
    relay_until(100)
    chunk(46.5, 0.6, (11,), (((1, 2), (-1, 2)),), per=4)
    chunk(51, 0.75, (5,), (((2, 0), (2, -1)), ((2, 1), (2, 2))), last=True, per=8)
    for c, when in started:
        if when is None:
            c.wait_send()
        else:
            pl.when(when)(c.wait_send)


def on_device(queries, resp_kv, resp_segments, prefix_kv, tile_plan, prompt_lengths):
    anywhere = pl.BlockSpec(memory_space=pl.ANY)
    inside = pl.BlockSpec(memory_space=VMEM)
    out = pl.pallas_call(
        main_kernel,
        out_shape=jax.ShapeDtypeStruct((ROWS, H * HD), jnp.bfloat16),
        in_specs=[pl.BlockSpec(memory_space=pltpu.SMEM)] * 2 + [anywhere] * 4,
        out_specs=inside,
        scratch_shapes=[
            VMEM((ROWS, H * HD), jnp.bfloat16),
            VMEM((4, TILE, WIDE), jnp.bfloat16),
            VMEM((4, TILE, WIDE), jnp.bfloat16),
            VMEM((4, 1, 128), jnp.int32),
            VMEM((32, 4, 1, 128), jnp.int32),
            VMEM((9, ROWS, WIDE), jnp.bfloat16),
            VMEM((9, 1, 128), jnp.int32),
            VMEM((32, 32, WIDE), jnp.bfloat16),
            VMEM((H, ROWS, 128), jnp.float32),
            VMEM((H, ROWS, 128), jnp.float32),
            VMEM((H, ROWS, 128), jnp.float32),
            VMEM((8, 512), jnp.float32),
            VMEM((8, ROWS, 128), jnp.float32),
            pltpu.SemaphoreType.DMA((NCOPY,)),
            pltpu.SemaphoreType.DMA((NCOPY,)),
            pltpu.SemaphoreType.DMA((6,)),
        ],
        compiler_params=pltpu.CompilerParams(
            collective_id=0, has_side_effects=True, vmem_limit_bytes=40 << 20
        ),
        name="attend",
    )(prompt_lengths, pltpu.with_memory_space_constraint(tile_plan.T, pltpu.HBM), *(pltpu.with_memory_space_constraint(t, pltpu.HBM) for t in (queries[0], resp_kv[0], resp_segments, prefix_kv)))
    return out[None]


def solution(mesh):
    return jax.shard_map(
        on_device,
        mesh=mesh,
        in_specs=(
            P("prompt", "resp", None),
            P("prompt", "resp", None),
            P("prompt", "resp"),
            P(("prompt", "resp"), None, None),
            P(("prompt", "resp"), None),
            P("prompt"),
        ),
        out_specs=P("prompt", "resp", None),
        check_vma=False,
    )
```
